512 devices in a mesh: wide: 128 (over z, y, core), pair: 4 (over x).
Axes of the slice: x: 4, y: 4, z: 16, core: 2. Of those that a mesh axis runs over, the one named last changes fastest.
Arguments:
- three_center: bfloat16 [512, 8, 1024], P('wide'), may hold values from -0.3125 to 0.3125
- occ_green: bfloat16 [512, 128, 8, 8], P('wide', 'pair'), may hold values from -2 to 2
- virt_green: bfloat16 [512, 128, 8, 8], P('wide', 'pair'), may hold values from -2 to 2
- occ_column: int32 [512, 128], P('wide', 'pair'), may hold values from 0 to 511, as said below
- partner_live: int32 [512, 128], P('wide', 'pair'), may hold values 0 or 1
Outputs:
- response: float32 [128, 128], P('pair')
The draws below stay inside these ranges and needn't reach their ends.
Inputs may be any that keep to these rules, and one draw needn't show every extreme that they name: `occ_column`: for each index of pair and each index w of wide, the slots of that group on the 4 atom blocks w * 4 to w * 4 + 3 name partner blocks k such that no value of k // 4 occurs more than 2 times, and some value occurs exactly 2 times.
All inputs are finite; a program needn't handle non-finite values. No bound on the sum of `partner_live` on one device may be relied on, other than what follows from the above.
Results may differ from the reference program's by a relative error of at most 0.004.
Values may be sent and summed in bfloat16 or wider, within the bound.
A program may use at most 64 MiB of HBM per device.

```python
import jax
import jax.numpy as jnp
from jax import lax

BS = 8
PB = 128
AD = 4
CAP = 2
KP = 32
KO = 128
NA = 512
N_PAIR = 4


def draw_occ_column(key, part):
    owner_total = NA // AD
    group_total = KO // KP
    slot_total = owner_total * CAP
    unit_total = AD * KP
    slot_owner = jnp.repeat(jnp.arange(owner_total, dtype=jnp.int32), CAP)
    favour = jax.random.randint(jax.random.fold_in(key, 11), (owner_total,), 0, 2) * 2048

    def one_group(index):
        subkey = jax.random.fold_in(key, index + 100)
        key_list = jax.random.split(subkey, 4)
        score = jax.random.randint(key_list[0], (slot_total,), 0, 4096) + favour[slot_owner]
        forced = jax.random.randint(key_list[1], (), 0, owner_total)
        score = jnp.where(slot_owner == forced, 8192, score)
        distinct = score * slot_total + jnp.arange(slot_total, dtype=jnp.int32)
        _, chosen = lax.top_k(distinct, unit_total)
        owners = slot_owner[chosen]
        owners = owners[jax.random.permutation(key_list[2], unit_total)]
        local_row = jax.random.randint(key_list[3], (unit_total,), 0, AD)
        return owners * AD + local_row
    table = jax.vmap(one_group)(jnp.arange(owner_total * group_total, dtype=jnp.int32))
    table = table.reshape(owner_total, group_total, AD, KP).transpose(0, 2, 1, 3)
    return table.reshape(owner_total * AD, group_total * KP).astype(jnp.int32)


def with_ends(result, stream_key, least, top_value):
    extent = result.shape
    spot = [jax.random.randint(jax.random.fold_in(stream_key, axis), (), 0, extent[axis]) for axis in range(len(extent))]
    result = result.at[tuple(spot)].set(least)
    longest = extent.index(max(extent))
    spot[longest] = (spot[longest] + 1) % extent[longest]
    return result.at[tuple(spot)].set(top_value)


def levels(own_key, dims, pieces, smallest, top_value):
    def one(axis_at, shards_of):
        heights = jax.random.uniform(jax.random.fold_in(jax.random.fold_in(own_key, 6), axis_at), (shards_of,), jnp.float32, smallest / len(pieces), top_value / len(pieces))
        return jnp.repeat(jnp.exp(heights), dims[axis_at] // shards_of).reshape((-1,) + (1,) * (len(dims) - axis_at - 1))

    loudness = one(*pieces[0])
    for cut in pieces[1:]:
        loudness = loudness * one(*cut)
    return loudness


def normal_values(own_key, shape, scale, bound, shards=(), held_as=jnp.bfloat16):
    array = scale * jax.random.normal(own_key, shape, jnp.float32)
    if shards:
        array = array * levels(own_key, shape, shards, -0.22, 0.18)
    return jnp.clip(array, -bound, bound).astype(held_as)


def setup_inputs(seed: int = 0) -> dict:
    keys = jax.random.split(jax.random.key(seed), 6)
    three_center = normal_values(keys[0], (NA, BS, BS * PB), ((KO * NA * BS * BS) ** -0.25), 0.3125, ((0, 128),))
    occ_green = normal_values(keys[1], (NA, KO, BS, BS), BS ** -0.5, 2.0, ((0, 128), (1, 4)))
    virt_green = normal_values(keys[2], (NA, KO, BS, BS), BS ** -0.5, 2.0, ((0, 128), (1, 4)))
    occ_column = draw_occ_column(jax.random.fold_in(keys[5], 71), 0)
    partner_live = with_ends((jax.random.randint(keys[4], (NA, KO), 0, 5) < 4).astype(jnp.int32), jax.random.fold_in(keys[4], 1), 0, 1)
    return {"three_center": three_center, "occ_green": occ_green, "virt_green": virt_green, "occ_column": occ_column, "partner_live": partner_live}


def round_trip(values):
    return lax.optimization_barrier(values.astype(jnp.bfloat16)).astype(jnp.float32)


def reference(three_center, occ_green, virt_green, occ_column, partner_live):
    atom_count = three_center.shape[0]
    blocks = three_center.astype(jnp.float32)
    flat_blocks = blocks.reshape(atom_count * BS * BS, PB)
    response = jnp.zeros((PB, PB), jnp.float32)
    for pair_group in range(N_PAIR):
        def add_slot(partner_sum, slot):
            occ_block = lax.dynamic_index_in_dim(occ_green, slot, 1, False).astype(jnp.float32)
            virt_block = lax.dynamic_index_in_dim(virt_green, slot, 1, False).astype(jnp.float32)
            target = lax.dynamic_index_in_dim(occ_column, slot, 1, False).astype(jnp.int32)
            weight = lax.dynamic_index_in_dim(partner_live, slot, 1, False).astype(jnp.float32)
            occupied_part = jnp.einsum("anl,anx->alx", occ_block, blocks, precision=lax.Precision.HIGHEST)
            occupied_part = round_trip(occupied_part * weight[:, None, None])
            both_part = jnp.einsum("alnp,ans->alsp", occupied_part.reshape(atom_count, BS, BS, PB), virt_block, precision=lax.Precision.HIGHEST)
            both_part = round_trip(both_part)
            partner_sum = partner_sum.at[target].add(both_part.reshape(atom_count, BS * BS * PB))
            return partner_sum, None

        start = jnp.zeros((atom_count, BS * BS * PB), jnp.float32)
        slot_list = jnp.arange(KP, dtype=jnp.int32) + pair_group * KP
        partner_sum, _ = lax.scan(add_slot, start, slot_list)
        summed = partner_sum.reshape(atom_count * BS * BS, PB)
        response = response + jnp.dot(summed.T, flat_blocks, precision=lax.Precision.HIGHEST, preferred_element_type=jnp.float32)
    return response
```

```python
import jax
import jax.numpy as jnp
from jax import lax
from jax.experimental import pallas as pl
from jax.experimental.pallas import tpu as pltpu
from jax.sharding import PartitionSpec as P

NZ, NY, NC, NX = 16, 4, 2, 4
PEERS = NX * NY
OWN = 8
CAP = 2
AD = 4
BB = 64
PB = 128
MESH = pl.DeviceIdType.MESH
F32 = jnp.float32
BF16 = jnp.bfloat16
NT = (((1,), (1,)), ((), ()))
TN = (((0,), (0,)), ((), ()))


def iota(shape, dim):
    return lax.broadcasted_iota(jnp.int32, shape, dim)


def one_hot(cond):
    return jnp.where(cond, 1.0, 0.0)


def kernel(
    t_ref, occ_ref, virt_ref, col_ref, live_ref, out_ref,
    sbuf, rbuf, ta, tk, meta_v, meta_s, oo, vv, lhs, rhs, yb, r3, g1, mine, g2, fin, g3,
    u_send, u_recv, a_send, a_recv, ka_send, kb_send, kc_send, k_recv, kc_recv,
    p1_send, p1_recv, p2_send, p2_recv, p3_send, p3_recv, loc,
):
    w = lax.axis_index("wide")
    x = lax.axis_index("pair")
    z = w // (NY * NC)
    y = (w // NC) % NY
    c = w % NC

    def place(zz, yy, cc):
        return zz * (NY * NC) + yy * NC + cc

    def remote(src, dst, ss, rs, wide, pair):
        return pltpu.make_async_remote_copy(
            src_ref=src, dst_ref=dst, send_sem=ss, recv_sem=rs, device_id=(wide, pair), device_id_type=MESH
        )

    barrier = pltpu.get_barrier_semaphore()
    for dx in range(NX):
        for dy in range(NY):
            for dc in range(NC):
                if dx + dy + dc:
                    pl.semaphore_signal(
                        barrier, inc=1, device_id_type=MESH,
                        device_id=(place(z, (y + dy) % NY, (c + dc) % NC), (x + dx) % NX),
                    )
    for dz in range(1, NZ):
        pl.semaphore_signal(
            barrier, inc=1, device_id_type=MESH, device_id=(place((z + dz) % NZ, y, c), x)
        )

    own_ta = pltpu.make_async_copy(t_ref, ta.at[pl.ds(0, AD * BB)], loc.at[0])
    own_ta.start()

    tri = one_hot(iota((32, 32), 0) < iota((32, 32), 1)).astype(BF16)
    base = jnp.zeros((PEERS * OWN, 1), F32)
    packed = jnp.zeros((PEERS * OWN * CAP, PB), F32)
    codes = jnp.zeros((PEERS, PB), F32)
    for a in range(AD):
        k = col_ref[a : a + 1, :]
        owner = k // AD
        zk, yk, ck = owner // (NY * NC), (owner // NC) % NY, owner % NC
        dest = (zk % NX) * NY + yk
        ow = (zk // NX) * NC + ck
        hit = one_hot(iota((PEERS * OWN, 32), 0) == dest * OWN + ow)
        hit16 = hit.astype(BF16)
        before = jnp.dot(hit16, tri, preferred_element_type=F32) + base
        base = base + jnp.sum(hit, axis=1, keepdims=True)
        rank = jnp.sum(hit * before, axis=0, keepdims=True).astype(jnp.int32)
        inner = rank * OWN + ow
        take = (iota((PEERS * OWN * CAP, 32), 0) == dest * (OWN * CAP) + inner) & (live_ref[a : a + 1, :] > 0)
        units = jnp.concatenate([occ_ref[a], virt_ref[a]], axis=0)
        packed += lax.dot_general(one_hot(take).astype(BF16), units, NT, preferred_element_type=F32)
        code = jnp.where(iota((PEERS, 32), 0) == dest, (a * AD + k % AD).astype(F32), 0.0).astype(BF16)
        spot = one_hot(iota((PB, 32), 0) == inner).astype(BF16)
        codes += lax.dot_general(code, spot, NT, preferred_element_type=F32)
    for j in range(PEERS):
        sbuf[j, 0:16, :] = packed[j * 16 : (j + 1) * 16].astype(BF16)
        sbuf[j, 16:32, :] = jnp.broadcast_to(codes[j : j + 1], (16, PB)).astype(BF16)

    pl.semaphore_wait(barrier, PEERS * NC - 1 + NZ - 1)

    offsets = [(dx, dy) for dx in range(NX) for dy in range(NY)]
    sends = []
    for d, (dx, dy) in enumerate(offsets):
        if d:
            xt, yt = (x + dx) % NX, (y + dy) % NY
            copy = remote(sbuf.at[xt * NY + yt], rbuf.at[d], u_send.at[d], u_recv.at[d], place(z, yt, c), xt)
            copy.start()
            sends.append(copy)
    own_units = pltpu.make_async_copy(sbuf.at[x * NY + y], rbuf.at[0], loc.at[1])
    own_units.start()

    arrivals = []
    for dy in range(1, NY):
        copy = remote(
            t_ref, ta.at[pl.ds(dy * AD * BB, AD * BB)], a_send.at[dy], a_recv.at[dy], place(z, (y + dy) % NY, c), x
        )
        copy.start()
        arrivals.append(copy)
        sends.append(copy)

    phase = (z + NZ - x) % NX
    source = (z + NZ - jnp.where(phase == 3, -1, phase)) % NZ
    qs = source // NX

    def spread(i, src, to_z):
        row = ((qs + NX - i) % NX) * NC + c
        if to_z:
            for n, dz in enumerate((1, NZ - 1, 2)):
                remote(
                    src, tk.at[row], kb_send.at[i * 3 + n], k_recv.at[i], place((z + dz) % NZ, y, c), x
                ).start()
        remote(src, tk.at[row], kc_send.at[i], kc_recv.at[i], place(z, y, 1 - c), x).start()

    def block(i):
        return tk.at[((qs + NX - i) % NX) * NC + c]

    def other(i):
        return tk.at[((qs + NX - i) % NX) * NC + 1 - c]

    own_tk = pltpu.make_async_copy(t_ref, block(0), loc.at[2])

    @pl.when(phase == 0)
    def _():
        own_tk.start()
        for i in range(1, NX):
            remote(t_ref, block(0), ka_send.at[i], k_recv.at[i], place((z + NX * i) % NZ, y, c), x).start()
        spread(0, t_ref, True)

    own_units.wait()
    for d in range(1, PEERS):
        remote(sbuf.at[0], rbuf.at[d], u_send.at[d], u_recv.at[d], w, x).wait_recv()
    for d in range(PEERS):
        meta_v[d : d + 1, :] = rbuf[d, 16:17, :].astype(F32).astype(jnp.int32)
    to_smem = pltpu.make_async_copy(meta_v, meta_s, loc.at[3])
    to_smem.start()
    got = rbuf[:, 0:16, :].astype(F32).reshape(PEERS, CAP, OWN, PB)
    both = jnp.concatenate(
        [got[:, 0].reshape(PEERS * OWN, PB).astype(BF16), got[:, 1].reshape(PEERS * OWN, PB).astype(BF16)], axis=1
    )
    row = iota((CAP * PB, PB), 0)
    lane = iota((CAP * PB, PB), 1)
    for f, arr in enumerate((oo, vv)):
        pick = (lane % 8) if f == 0 else (lane // 8) % 8
        target = (lane // BB) * PB + f * BB + pick * 8
        for g in range(8):
            sel = one_hot(row == target + g).astype(BF16)
            arr[:, g, :] = jnp.dot(both, sel, preferred_element_type=F32)
    to_smem.wait()

    @pl.when(phase == 0)
    def _():
        for i in range(1, NX):
            remote(t_ref, block(i), ka_send.at[i], k_recv.at[i], w, x).wait_recv()
            spread(i, block(i), True)

    own_ta.wait()
    for copy in arrivals:
        copy.wait_recv()

    def one_owner(ow, carry):
        low = iota((8, PB), 1) < BB
        for d, (dx, dy) in enumerate(offsets):
            c0, c1 = meta_s[d, ow], meta_s[d, OWN + ow]
            kv = jnp.where(low, c0 & 3, c1 & 3)
            o = oo[d * OWN + ow]
            v = vv[d * OWN + ow]
            vs = [jnp.broadcast_to(v[s : s + 1, :], (8, PB)) for s in range(8)]
            for kk in range(AD):
                ok = jnp.where(kv == kk, o, 0.0)
                for s in range(0, 8, 2):
                    m = jnp.concatenate([ok * vs[s], ok * vs[s + 1]], axis=0).astype(BF16)
                    lhs[kk * BB + s * 8 : kk * BB + s * 8 + 16, d * PB : (d + 1) * PB] = m
            for cap, code in ((0, c0), (1, c1)):
                atoms = [ta[(dy * AD + a) * BB : (dy * AD + a + 1) * BB, :] for a in range(AD)]
                low_pair = jnp.where((code & 4) == 0, atoms[0], atoms[1])
                high_pair = jnp.where((code & 4) == 0, atoms[2], atoms[3])
                rhs[d * PB + cap * BB : d * PB + (cap + 1) * BB, :] = jnp.where(
                    (code & 8) == 0, low_pair, high_pair
                )
        yb[pl.ds(pl.multiple_of(ow * AD * BB, AD * BB), AD * BB), :] = jnp.dot(
            lhs[...], rhs[...], preferred_element_type=F32
        )
        return carry

    lax.fori_loop(0, OWN // 2, one_owner, 0)

    @pl.when(phase != 0)
    def _():
        for i in range(NX):
            remote(t_ref, block(i), ka_send.at[i], k_recv.at[i], w, x).wait_recv()
            spread(i, block(i), False)

    lax.fori_loop(OWN // 2, OWN, one_owner, 0)

    @pl.when(phase == 0)
    def _():
        own_tk.wait()

    for i in range(NX):
        remote(t_ref, other(i), kc_send.at[i], kc_recv.at[i], w, x).wait_recv()

    total = jnp.zeros((2 * PB, PB), F32)
    for ow in range(OWN):
        yy = yb[ow * AD * BB : (ow + 1) * AD * BB, :]
        hi = yy.astype(BF16)
        lo = (yy - hi.astype(F32)).astype(BF16)
        total += lax.dot_general(
            jnp.concatenate([hi, lo], axis=1), tk[ow], TN, preferred_element_type=F32
        )
    part = total[:PB] + total[PB:]
    for xx in range(NX):
        for n in range(NY * NC):
            r3[xx, n] = part[xx * 32 + n * 4 : xx * 32 + n * 4 + 4]

    waits = []
    d = 0
    for dx in range(NX):
        for dy in range(NY):
            for dc in range(NC):
                if d:
                    xt, yt, ct = (x + dx) % NX, (y + dy) % NY, (c + dc) % NC
                    copy = remote(
                        r3.at[xt, yt * NC + ct], g1.at[d], p1_send.at[d], p1_recv.at[d], place(z, yt, ct), xt
                    )
                    copy.start()
                    waits.append(copy)
                d += 1
    total4 = r3[x, y * NC + c]
    for copy in waits:
        copy.wait_recv()
    sends += waits
    for d in range(1, PEERS * NC):
        total4 += g1[d]
    mine[...] = total4

    waits = []
    for dz in range(1, NZ):
        copy = remote(mine, g2.at[z], p2_send.at[dz], p2_recv.at[dz], place((z + dz) % NZ, y, c), x)
        copy.start()
        waits.append(copy)
    g2[z] = total4
    for copy in waits:
        copy.wait_recv()
    sends += waits
    total4 = g2[0]
    for n in range(1, NZ):
        total4 += g2[n]
    fin[...] = total4

    waits = []
    here = y * NC + c
    for n in range(1, NY * NC):
        dy, dc = n // NC, n % NC
        copy = remote(
            fin, g3.at[here], p3_send.at[n], p3_recv.at[n], place(z, (y + dy) % NY, (c + dc) % NC), x
        )
        copy.start()
        waits.append(copy)
    g3[here] = total4
    for copy in waits:
        copy.wait_recv()
    sends += waits
    for n in range(NY * NC):
        out_ref[n * 4 : (n + 1) * 4, :] = g3[n]

    for copy in sends:
        copy.wait_send()
    for i in range(NX):
        remote(t_ref, block(i), kc_send.at[i], kc_recv.at[i], w, x).wait_send()

    @pl.when(phase == 0)
    def _():
        for i in range(1, NX):
            remote(t_ref, block(i), ka_send.at[i], k_recv.at[i], w, x).wait_send()
        for i in range(3 * NX):
            remote(t_ref, block(0), kb_send.at[i], k_recv.at[0], w, x).wait_send()


def local(three_center, occ_green, virt_green, occ_column, partner_live):
    t = three_center.reshape(AD, 8, 8, PB).transpose(0, 2, 1, 3).reshape(AD * BB, PB)
    occ = occ_green.transpose(0, 2, 3, 1).reshape(AD, BB, 32)
    virt = virt_green.transpose(0, 2, 3, 1).reshape(AD, BB, 32)
    vmem = pl.BlockSpec(memory_space=pltpu.VMEM)
    dma = pltpu.SemaphoreType.DMA
    return pl.pallas_call(
        kernel,
        out_shape=jax.ShapeDtypeStruct((32, PB), F32),
        in_specs=[vmem] * 5,
        out_specs=vmem,
        scratch_shapes=[
            pltpu.VMEM((PEERS, 32, PB), BF16),
            pltpu.VMEM((PEERS, 32, PB), BF16),
            pltpu.VMEM((NY * AD * BB, PB), BF16),
            pltpu.VMEM((OWN, AD * BB, PB), BF16),
            pltpu.VMEM((PEERS, PB), jnp.int32),
            pltpu.SMEM((PEERS, PB), jnp.int32),
            pltpu.VMEM((PEERS * OWN, 8, PB), F32),
            pltpu.VMEM((PEERS * OWN, 8, PB), F32),
            pltpu.VMEM((AD * BB, PEERS * PB), BF16),
            pltpu.VMEM((PEERS * PB, PB), BF16),
            pltpu.VMEM((OWN * AD * BB, PB), F32),
            pltpu.VMEM((NX, NY * NC, 4, PB), F32),
            pltpu.VMEM((PEERS * NC, 4, PB), F32),
            pltpu.VMEM((4, PB), F32),
            pltpu.VMEM((NZ, 4, PB), F32),
            pltpu.VMEM((4, PB), F32),
            pltpu.VMEM((NY * NC, 4, PB), F32),
            dma((PEERS,)), dma((PEERS,)),
            dma((NY,)), dma((NY,)),
            dma((NX,)), dma((3 * NX,)), dma((NX,)), dma((NX,)), dma((NX,)),
            dma((PEERS * NC,)), dma((PEERS * NC,)),
            dma((NZ,)), dma((NZ,)),
            dma((NY * NC,)), dma((NY * NC,)),
            dma((4,)),
        ],
        compiler_params=pltpu.CompilerParams(
            collective_id=0, has_side_effects=True, vmem_limit_bytes=32 * 1024 * 1024
        ),
    )(t, occ, virt, occ_column, partner_live)


def solution(mesh):
    placed = (
        P("wide", None, None),
        P("wide", "pair", None, None),
        P("wide", "pair", None, None),
        P("wide", "pair"),
        P("wide", "pair"),
    )
    return jax.shard_map(
        local, mesh=mesh, in_specs=placed, out_specs=P("pair", None), check_vma=False
    )
```

```python
import jax
import jax.numpy as jnp
from jax import lax
from jax.experimental import pallas as pl
from jax.experimental.pallas import tpu as pltpu
from jax.sharding import PartitionSpec as P

NZ, NY, NC, NX = 16, 4, 2, 4
PEERS = NX * NY
OWN = 8
CAP = 2
AD = 4
BB = 64
PB = 128
MESH = pl.DeviceIdType.MESH
F32 = jnp.float32
BF16 = jnp.bfloat16
NT = (((1,), (1,)), ((), ()))
TN = (((0,), (0,)), ((), ()))


def iota(shape, dim):
    return lax.broadcasted_iota(jnp.int32, shape, dim)


def one_hot(cond):
    return jnp.where(cond, 1.0, 0.0)


def kernel(
    t_hbm, occ_hbm, virt_hbm, col_hbm, live_hbm, out_ref,
    occ_ref, virt_ref, col_ref, live_ref, sbuf, rbuf, ta, tk, meta_v, meta_s, oo, vv, lhs, rhs, yb, r3, g1, mine, g2, fin, g3,
    u_send, u_recv, a_send, a_recv, ka_send, kb_send, kc_send, k_recv, kc_recv,
    p1_send, p1_recv, p2_send, p2_recv, p3_send, p3_recv, loc,
):
    w = lax.axis_index("wide")
    x = lax.axis_index("pair")
    z = w // (NY * NC)
    y = (w // NC) % NY
    c = w % NC

    def place(zz, yy, cc):
        return zz * (NY * NC) + yy * NC + cc

    def remote(src, dst, ss, rs, wide, pair):
        return pltpu.make_async_remote_copy(
            src_ref=src, dst_ref=dst, send_sem=ss, recv_sem=rs, device_id=(wide, pair), device_id_type=MESH
        )

    t_ref = ta.at[pl.ds(0, AD * BB)]
    load_t = pltpu.make_async_copy(t_hbm, t_ref, loc.at[0])
    loads = [
        pltpu.make_async_copy(src, dst, loc.at[4 + n])
        for n, (src, dst) in enumerate(
            ((col_hbm, col_ref), (live_hbm, live_ref), (occ_hbm, occ_ref), (virt_hbm, virt_ref))
        )
    ]
    for copy in loads:
        copy.start()
    load_t.start()

    greeted = [(z, (y + dy) % NY, c, (x + dx) % NX) for dx in range(NX) for dy in range(NY) if dx + dy]
    greeted += [(z, y, 1 - c, x)]
    greeted += [((z + dz) % NZ, y, c, x) for dz in (1, NZ - 1, 2, NZ - 2, NX, NZ - NX)]
    barrier = pltpu.get_barrier_semaphore()
    for zz, yy, cc, xx in greeted:
        pl.semaphore_signal(barrier, inc=1, device_id=(place(zz, yy, cc), xx), device_id_type=MESH)
    for copy in loads:
        copy.wait()

    tri = one_hot(iota((32, 32), 0) < iota((32, 32), 1)).astype(BF16)
    base = jnp.zeros((PEERS * OWN, 1), F32)
    packed = jnp.zeros((PEERS * OWN * CAP, PB), F32)
    codes = jnp.zeros((PEERS, PB), F32)
    for a in range(AD):
        k = col_ref[a : a + 1, :]
        owner = k // AD
        zk, yk, ck = owner // (NY * NC), (owner // NC) % NY, owner % NC
        dest = (zk % NX) * NY + yk
        ow = (zk // NX) * NC + ck
        hit = one_hot(iota((PEERS * OWN, 32), 0) == dest * OWN + ow)
        hit16 = hit.astype(BF16)
        before = jnp.dot(hit16, tri, preferred_element_type=F32) + base
        base = base + jnp.sum(hit, axis=1, keepdims=True)
        rank = jnp.sum(hit * before, axis=0, keepdims=True).astype(jnp.int32)
        inner = rank * OWN + ow
        take = (iota((PEERS * OWN * CAP, 32), 0) == dest * (OWN * CAP) + inner) & (live_ref[a : a + 1, :] > 0)
        units = jnp.concatenate([occ_ref[a], virt_ref[a]], axis=0)
        packed += lax.dot_general(one_hot(take).astype(BF16), units, NT, preferred_element_type=F32)
        code = jnp.where(iota((PEERS, 32), 0) == dest, (a * AD + k % AD).astype(F32), 0.0).astype(BF16)
        spot = one_hot(iota((PB, 32), 0) == inner).astype(BF16)
        codes += lax.dot_general(code, spot, NT, preferred_element_type=F32)
    for j in range(PEERS):
        sbuf[j, 0:16, :] = packed[j * 16 : (j + 1) * 16].astype(BF16)
        sbuf[j, 16:32, :] = jnp.broadcast_to(codes[j : j + 1], (16, PB)).astype(BF16)

    pl.semaphore_wait(barrier, len(greeted))

    offsets = [(dx, dy) for dx in range(NX) for dy in range(NY)]
    sends = []
    for d, (dx, dy) in enumerate(offsets):
        if d:
            xt, yt = (x + dx) % NX, (y + dy) % NY
            copy = remote(sbuf.at[xt * NY + yt], rbuf.at[d], u_send.at[d], u_recv.at[d], place(z, yt, c), xt)
            copy.start()
            sends.append(copy)
    own_units = pltpu.make_async_copy(sbuf.at[x * NY + y], rbuf.at[0], loc.at[1])
    own_units.start()

    load_t.wait()
    arrivals = []
    for dy in range(1, NY):
        copy = remote(
            t_ref, ta.at[pl.ds(dy * AD * BB, AD * BB)], a_send.at[dy], a_recv.at[dy], place(z, (y + dy) % NY, c), x
        )
        copy.start()
        arrivals.append(copy)
        sends.append(copy)

    phase = (z + NZ - x) % NX
    way = 1 - 2 * c
    shift = jnp.where(phase == 2, 2 * way, jnp.where(phase == 3, -1, phase))
    qs = ((z + NZ - shift) % NZ) // NX

    def block(i, core=c):
        return tk.at[((qs + NX - i) % NX) * NC + core]

    def got_block(i):
        remote(t_ref, block(i), ka_send.at[0], k_recv.at[i], w, x).wait_recv()

    def to_z(src, dst, ss, rs, dz):
        remote(src, dst, ss, rs, place((z + NZ + dz) % NZ, y, c), x).start()

    def around(i, src):
        for n, dz in enumerate((1, -1, 2 * way)):
            to_z(src, block(i), kb_send.at[i * 3 + n], k_recv.at[i], dz)

    def across(i, src):
        remote(src, block(i), kc_send.at[i], kc_recv.at[i], place(z, y, 1 - c), x).start()

    own_tk = pltpu.make_async_copy(t_ref, block(0), loc.at[2])

    @pl.when(phase == 0)
    def _():
        to_z(t_ref, block(0), ka_send.at[0], k_recv.at[1], NX)
        to_z(t_ref, block(0), ka_send.at[1], k_recv.at[3], -NX)
        around(0, t_ref)
        across(0, t_ref)
        own_tk.start()

    own_units.wait()
    for d in range(1, PEERS):
        remote(sbuf.at[0], rbuf.at[d], u_send.at[d], u_recv.at[d], w, x).wait_recv()
    for d in range(PEERS):
        meta_v[d : d + 1, :] = rbuf[d, 16:17, :].astype(F32).astype(jnp.int32)
    to_smem = pltpu.make_async_copy(meta_v, meta_s, loc.at[3])
    to_smem.start()
    got = rbuf[:, 0:16, :].astype(F32).reshape(PEERS, CAP, OWN, PB)
    both = jnp.concatenate(
        [got[:, 0].reshape(PEERS * OWN, PB).astype(BF16), got[:, 1].reshape(PEERS * OWN, PB).astype(BF16)], axis=1
    )
    row = iota((CAP * PB, PB), 0)
    lane = iota((CAP * PB, PB), 1)
    for f, arr in enumerate((oo, vv)):
        pick = (lane % 8) if f == 0 else (lane // 8) % 8
        target = (lane // BB) * PB + f * BB + pick * 8
        for g in range(8):
            sel = one_hot(row == target + g).astype(BF16)
            arr[:, g, :] = jnp.dot(both, sel, preferred_element_type=F32)
    to_smem.wait()

    @pl.when(phase == 0)
    def _():
        got_block(1)
        got_block(3)
        relay = block(1 + 2 * c)
        to_z(relay, relay, ka_send.at[2], k_recv.at[2], NX * way)
        for i in (1, 3):
            around(i, block(i))
            across(i, block(i))

    for copy in arrivals:
        copy.wait_recv()

    def one_owner(ow, carry):
        low = iota((8, PB), 1) < BB
        for d, (dx, dy) in enumerate(offsets):
            c0, c1 = meta_s[d, ow], meta_s[d, OWN + ow]
            kv = jnp.where(low, c0 & 3, c1 & 3)
            o = oo[d * OWN + ow]
            v = vv[d * OWN + ow]
            vs = [jnp.broadcast_to(v[s : s + 1, :], (8, PB)) for s in range(8)]
            for kk in range(AD):
                ok = jnp.where(kv == kk, o, 0.0)
                for s in range(0, 8, 2):
                    m = jnp.concatenate([ok * vs[s], ok * vs[s + 1]], axis=0).astype(BF16)
                    lhs[kk * BB + s * 8 : kk * BB + s * 8 + 16, d * PB : (d + 1) * PB] = m
            for cap, code in ((0, c0), (1, c1)):
                atoms = [ta[(dy * AD + a) * BB : (dy * AD + a + 1) * BB, :] for a in range(AD)]
                low_pair = jnp.where((code & 4) == 0, atoms[0], atoms[1])
                high_pair = jnp.where((code & 4) == 0, atoms[2], atoms[3])
                rhs[d * PB + cap * BB : d * PB + (cap + 1) * BB, :] = jnp.where(
                    (code & 8) == 0, low_pair, high_pair
                )
        yb[pl.ds(pl.multiple_of(ow * AD * BB, AD * BB), AD * BB), :] = jnp.dot(
            lhs[...], rhs[...], preferred_element_type=F32
        )
        return carry

    lax.fori_loop(0, OWN // 2, one_owner, 0)

    @pl.when(phase == 0)
    def _():
        got_block(2)
        around(2, block(2))
        across(2, block(2))

    @pl.when(phase != 0)
    def _():
        for i in (0, 1, 3):
            got_block(i)
            across(i, block(i))

    lax.fori_loop(OWN // 2, OWN, one_owner, 0)

    @pl.when(phase != 0)
    def _():
        got_block(2)
        across(2, block(2))

    @pl.when(phase == 0)
    def _():
        own_tk.wait()

    for i in range(NX):
        remote(t_ref, block(i, 1 - c), kc_send.at[i], kc_recv.at[i], w, x).wait_recv()

    total = jnp.zeros((2 * PB, PB), F32)
    for ow in range(OWN):
        yy = yb[ow * AD * BB : (ow + 1) * AD * BB, :]
        hi = yy.astype(BF16)
        lo = (yy - hi.astype(F32)).astype(BF16)
        total += lax.dot_general(
            jnp.concatenate([hi, lo], axis=1), tk[ow], TN, preferred_element_type=F32
        )
    part = total[:PB] + total[PB:]
    for xx in range(NX):
        for n in range(NY * NC):
            r3[xx, n] = part[xx * 32 + n * 4 : xx * 32 + n * 4 + 4]

    waits = []
    d = 0
    for dx in range(NX):
        for dy in range(NY):
            for dc in range(NC):
                if d:
                    xt, yt, ct = (x + dx) % NX, (y + dy) % NY, (c + dc) % NC
                    copy = remote(
                        r3.at[xt, yt * NC + ct], g1.at[d], p1_send.at[d], p1_recv.at[d], place(z, yt, ct), xt
                    )
                    copy.start()
                    waits.append(copy)
                d += 1
    total4 = r3[x, y * NC + c]
    for copy in waits:
        copy.wait_recv()
    sends += waits
    for d in range(1, PEERS * NC):
        total4 += g1[d]
    mine[...] = total4

    waits = []
    for dz in range(1, NZ):
        copy = remote(mine, g2.at[z], p2_send.at[dz], p2_recv.at[dz], place((z + dz) % NZ, y, c), x)
        copy.start()
        waits.append(copy)
    g2[z] = total4
    for copy in waits:
        copy.wait_recv()
    sends += waits
    total4 = g2[0]
    for n in range(1, NZ):
        total4 += g2[n]
    fin[...] = total4

    waits = []
    here = y * NC + c
    for n in range(1, NY * NC):
        dy, dc = n // NC, n % NC
        copy = remote(
            fin, g3.at[here], p3_send.at[n], p3_recv.at[n], place(z, (y + dy) % NY, (c + dc) % NC), x
        )
        copy.start()
        waits.append(copy)
    g3[here] = total4
    for copy in waits:
        copy.wait_recv()
    sends += waits
    for n in range(NY * NC):
        out_ref[n * 4 : (n + 1) * 4, :] = g3[n]

    for copy in sends:
        copy.wait_send()
    for i in range(NX):
        remote(t_ref, block(i), kc_send.at[i], kc_recv.at[i], w, x).wait_send()

    @pl.when(phase == 0)
    def _():
        for i in range(3):
            remote(t_ref, block(0), ka_send.at[i], k_recv.at[0], w, x).wait_send()
        for i in range(3 * NX):
            remote(t_ref, block(0), kb_send.at[i], k_recv.at[0], w, x).wait_send()


def local(three_center, occ_green, virt_green, occ_column, partner_live):
    t = three_center.reshape(AD, 8, 8, PB).transpose(0, 2, 1, 3).reshape(AD * BB, PB)
    occ = occ_green.transpose(0, 2, 3, 1).reshape(AD, BB, 32)
    virt = virt_green.transpose(0, 2, 3, 1).reshape(AD, BB, 32)
    vmem = pl.BlockSpec(memory_space=pltpu.VMEM)
    dma = pltpu.SemaphoreType.DMA
    return pl.pallas_call(
        kernel,
        out_shape=jax.ShapeDtypeStruct((32, PB), F32),
        in_specs=[pl.BlockSpec(memory_space=pltpu.HBM)] * 5,
        out_specs=vmem,
        scratch_shapes=[
            pltpu.VMEM((AD, BB, 32), BF16),
            pltpu.VMEM((AD, BB, 32), BF16),
            pltpu.VMEM((AD, 32), jnp.int32),
            pltpu.VMEM((AD, 32), jnp.int32),
            pltpu.VMEM((PEERS, 32, PB), BF16),
            pltpu.VMEM((PEERS, 32, PB), BF16),
            pltpu.VMEM((NY * AD * BB, PB), BF16),
            pltpu.VMEM((OWN, AD * BB, PB), BF16),
            pltpu.VMEM((PEERS, PB), jnp.int32),
            pltpu.SMEM((PEERS, PB), jnp.int32),
            pltpu.VMEM((PEERS * OWN, 8, PB), F32),
            pltpu.VMEM((PEERS * OWN, 8, PB), F32),
            pltpu.VMEM((AD * BB, PEERS * PB), BF16),
            pltpu.VMEM((PEERS * PB, PB), BF16),
            pltpu.VMEM((OWN * AD * BB, PB), F32),
            pltpu.VMEM((NX, NY * NC, 4, PB), F32),
            pltpu.VMEM((PEERS * NC, 4, PB), F32),
            pltpu.VMEM((4, PB), F32),
            pltpu.VMEM((NZ, 4, PB), F32),
            pltpu.VMEM((4, PB), F32),
            pltpu.VMEM((NY * NC, 4, PB), F32),
            dma((PEERS,)), dma((PEERS,)),
            dma((NY,)), dma((NY,)),
            dma((NX,)), dma((3 * NX,)), dma((NX,)), dma((NX,)), dma((NX,)),
            dma((PEERS * NC,)), dma((PEERS * NC,)),
            dma((NZ,)), dma((NZ,)),
            dma((NY * NC,)), dma((NY * NC,)),
            dma((8,)),
        ],
        compiler_params=pltpu.CompilerParams(
            collective_id=0, has_side_effects=True, vmem_limit_bytes=32 * 1024 * 1024
        ),
    )(*[pltpu.with_memory_space_constraint(v, pltpu.HBM) for v in (t, occ, virt, occ_column, partner_live)])


def solution(mesh):
    placed = (
        P("wide", None, None),
        P("wide", "pair", None, None),
        P("wide", "pair", None, None),
        P("wide", "pair"),
        P("wide", "pair"),
    )
    return jax.shard_map(
        local, mesh=mesh, in_specs=placed, out_specs=P("pair", None), check_vma=False
    )
```

```python
import jax
import jax.numpy as jnp
from jax import lax
from jax.experimental import pallas as pl
from jax.experimental.pallas import tpu as pltpu
from jax.sharding import PartitionSpec as P

NZ, NY, NC, NX = 16, 4, 2, 4
PEERS = NX * NY
OWN = 8
CAP = 2
AD = 4
BB = 64
PB = 128
MESH = pl.DeviceIdType.MESH
F32 = jnp.float32
FAR_FIRST = sorted(
    ((dx, dy) for dx in range(NX) for dy in range(NY)), key=lambda o: -min(o[0], NX - o[0]) - min(o[1], NY - o[1])
)
BF16 = jnp.bfloat16
NT = (((1,), (1,)), ((), ()))
TN = (((0,), (0,)), ((), ()))


def iota(shape, dim):
    return lax.broadcasted_iota(jnp.int32, shape, dim)


def one_hot(cond):
    return jnp.where(cond, 1.0, 0.0)


def kernel(
    t_hbm, occ_hbm, virt_hbm, col_hbm, live_hbm, out_ref,
    occ_ref, virt_ref, col_ref, live_ref, sbuf, rbuf, ta, tk, meta_v, meta_s, oo, vv, lhs0, lhs1, rhs0, rhs1, yb, r3, g1, mine, g2, fin, g3,
    u_send, u_recv, a_send, a_recv, ka_send, kb_send, kc_send, k_recv, kc_recv,
    p1_send, p1_recv, p2_send, p2_recv, p3_send, p3_recv, loc,
):
    w = lax.axis_index("wide")
    x = lax.axis_index("pair")
    z = w >> 3
    y = (w >> 1) & 3
    c = w & 1

    def at_x(n):
        return (x + n) & (NX - 1)

    def at_y(n):
        return (y + n) & (NY - 1)

    def at_z(n):
        return (z + NZ + n) & (NZ - 1)

    def place(zz, yy, cc):
        return zz * (NY * NC) + yy * NC + cc

    def remote(src, dst, ss, rs, wide, pair):
        return pltpu.make_async_remote_copy(
            src_ref=src, dst_ref=dst, send_sem=ss, recv_sem=rs, device_id=(wide, pair), device_id_type=MESH
        )

    t_ref = ta.at[pl.ds(0, AD * BB)]
    load_t = pltpu.make_async_copy(t_hbm, t_ref, loc.at[0])
    loads = [
        pltpu.make_async_copy(src, dst, loc.at[4 + n])
        for n, (src, dst) in enumerate(
            ((col_hbm, col_ref), (live_hbm, live_ref), (occ_hbm, occ_ref), (virt_hbm, virt_ref))
        )
    ]
    for copy in loads:
        copy.start()
    load_t.start()

    greeted = [(at_z(dz), y, c, x) for dz in (NX, -NX)]
    greeted += [(z, at_y(dy), c, at_x(dx)) for dx, dy in FAR_FIRST if dx + dy]
    greeted += [(at_z(dz), y, c, x) for dz in (2, -2, 1, -1)]
    greeted += [(z, y, 1 - c, x)]
    barrier = pltpu.get_barrier_semaphore()
    for zz, yy, cc, xx in greeted:
        pl.semaphore_signal(barrier, inc=1, device_id=(place(zz, yy, cc), xx), device_id_type=MESH)
    load_t.wait()
    pl.semaphore_wait(barrier, len(greeted))
    sends = []

    phase = (z + NZ - x) & (NX - 1)
    way = 1 - 2 * c
    shift = jnp.where(phase == 2, 2 * way, jnp.where(phase == 3, -1, phase))
    qs = at_z(-shift) >> 2

    def block(i, core=c):
        return tk.at[((qs + NX - i) & (NX - 1)) * NC + core]

    def got_block(i):
        remote(t_ref, block(i), ka_send.at[0], k_recv.at[i], w, x).wait_recv()

    def to_z(src, dst, ss, rs, dz):
        remote(src, dst, ss, rs, place(at_z(dz), y, c), x).start()

    def around(i, src):
        for n, dz in enumerate((1, -1, 2 * way)):
            to_z(src, block(i), kb_send.at[i * 3 + n], k_recv.at[i], dz)

    def across(i, src):
        remote(src, block(i), kc_send.at[i], kc_recv.at[i], place(z, y, 1 - c), x).start()

    own_tk = pltpu.make_async_copy(t_ref, block(0), loc.at[2])

    @pl.when(phase == 0)
    def _():
        to_z(t_ref, block(0), ka_send.at[0], k_recv.at[1], NX)
        to_z(t_ref, block(0), ka_send.at[1], k_recv.at[3], -NX)
        around(0, t_ref)
        across(0, t_ref)
        own_tk.start()

    for copy in loads:
        copy.wait()

    tri = one_hot(iota((32, 32), 0) < iota((32, 32), 1)).astype(BF16)
    base = jnp.zeros((PEERS * OWN, 1), F32)
    packed = jnp.zeros((PEERS * OWN * CAP, PB), F32)
    codes = jnp.zeros((PEERS, PB), F32)
    for a in range(AD):
        k = col_ref[a : a + 1, :]
        owner = k // AD
        zk, yk, ck = owner // (NY * NC), (owner // NC) % NY, owner % NC
        dest = (zk % NX) * NY + yk
        ow = (zk // NX) * NC + ck
        hit = one_hot(iota((PEERS * OWN, 32), 0) == dest * OWN + ow)
        hit16 = hit.astype(BF16)
        before = jnp.dot(hit16, tri, preferred_element_type=F32) + base
        base = base + jnp.sum(hit, axis=1, keepdims=True)
        rank = jnp.sum(hit * before, axis=0, keepdims=True).astype(jnp.int32)
        inner = rank * OWN + ow
        take = (iota((PEERS * OWN * CAP, 32), 0) == dest * (OWN * CAP) + inner) & (live_ref[a : a + 1, :] > 0)
        units = jnp.concatenate([occ_ref[a], virt_ref[a]], axis=0)
        packed += lax.dot_general(one_hot(take).astype(BF16), units, NT, preferred_element_type=F32)
        code = jnp.where(iota((PEERS, 32), 0) == dest, (a * AD + k % AD).astype(F32), 0.0).astype(BF16)
        spot = one_hot(iota((PB, 32), 0) == inner).astype(BF16)
        codes += lax.dot_general(code, spot, NT, preferred_element_type=F32)
    for j in range(PEERS):
        sbuf[j, 0:16, :] = packed[j * 16 : (j + 1) * 16].astype(BF16)
        sbuf[j, 16:32, :] = jnp.broadcast_to(codes[j : j + 1], (16, PB)).astype(BF16)

    offsets = [(dx, dy) for dx in range(NX) for dy in range(NY)]
    for dx, dy in FAR_FIRST:
        d = dx * NY + dy
        if d:
            xt, yt = at_x(dx), at_y(dy)
            copy = remote(sbuf.at[xt * NY + yt], rbuf.at[d], u_send.at[d], u_recv.at[d], place(z, yt, c), xt)
            copy.start()
            sends.append(copy)
    own_units = pltpu.make_async_copy(sbuf.at[x * NY + y], rbuf.at[0], loc.at[1])
    own_units.start()

    arrivals = []
    for dy in (2, 1, 3):
        copy = remote(
            t_ref, ta.at[pl.ds(dy * AD * BB, AD * BB)], a_send.at[dy], a_recv.at[dy], place(z, at_y(dy), c), x
        )
        copy.start()
        arrivals.append(copy)
        sends.append(copy)

    @pl.when(phase == 0)
    def _():
        first = 1 + 2 * c
        got_block(first)
        to_z(block(first), block(first), ka_send.at[2], k_recv.at[2], NX * way)
        around(first, block(first))
        across(first, block(first))
        got_block(NX - first)
        around(NX - first, block(NX - first))
        across(NX - first, block(NX - first))

    own_units.wait()
    for d in range(1, PEERS):
        remote(sbuf.at[0], rbuf.at[d], u_send.at[d], u_recv.at[d], w, x).wait_recv()
    for d in range(PEERS):
        meta_v[d : d + 1, :] = rbuf[d, 16:17, :].astype(F32).astype(jnp.int32)
    to_smem = pltpu.make_async_copy(meta_v, meta_s, loc.at[3])
    to_smem.start()
    got = rbuf[:, 0:16, :].astype(F32).reshape(PEERS, CAP, OWN, PB)
    both = jnp.concatenate(
        [got[:, 0].reshape(PEERS * OWN, PB).astype(BF16), got[:, 1].reshape(PEERS * OWN, PB).astype(BF16)], axis=1
    )
    row = iota((CAP * PB, PB), 0)
    lane = iota((CAP * PB, PB), 1)
    for f, arr in enumerate((oo, vv)):
        pick = (lane % 8) if f == 0 else (lane // 8) % 8
        target = (lane // BB) * PB + f * BB + pick * 8
        for g in range(8):
            sel = one_hot(row == target + g).astype(BF16)
            arr[:, g, :] = jnp.dot(both, sel, preferred_element_type=F32)
    to_smem.wait()

    for copy in arrivals:
        copy.wait_recv()

    @pl.when(phase == 0)
    def _():
        got_block(2)
        around(2, block(2))
        across(2, block(2))

    def build(ow, lhs, rhs):
        low = iota((8, PB), 1) < BB
        for dy in range(NY):
            atoms = [ta[(dy * AD + a) * BB : (dy * AD + a + 1) * BB, :] for a in range(AD)]
            for dx in range(NX):
                d = dx * NY + dy
                c0, c1 = meta_s[d, ow], meta_s[d, OWN + ow]
                kv = jnp.where(low, c0 & 3, c1 & 3)
                o = oo[d * OWN + ow]
                v = vv[d * OWN + ow]
                wide_v = [
                    jnp.concatenate([jnp.broadcast_to(v[s + n : s + n + 1, :], (8, PB)) for n in range(2)], axis=0)
                    for s in range(0, 8, 2)
                ]
                wide_v = [t.astype(BF16) for t in wide_v]
                for kk in range(AD):
                    ok = jnp.where(kv == kk, o, 0.0)
                    ok = jnp.concatenate([ok, ok], axis=0).astype(BF16)
                    for n, t in enumerate(wide_v):
                        lhs[kk * BB + n * 16 : kk * BB + n * 16 + 16, d * PB : (d + 1) * PB] = ok * t
                for cap, code in ((0, c0), (1, c1)):
                    low_pair = jnp.where((code & 4) == 0, atoms[0], atoms[1])
                    high_pair = jnp.where((code & 4) == 0, atoms[2], atoms[3])
                    rhs[d * PB + cap * BB : d * PB + (cap + 1) * BB, :] = jnp.where(
                        (code & 8) == 0, low_pair, high_pair
                    )

    def multiply(ow, lhs, rhs):
        yb[pl.ds(pl.multiple_of(ow * AD * BB, AD * BB), AD * BB), :] = jnp.dot(
            lhs[...], rhs[...], preferred_element_type=F32
        )

    def two_owners(n, carry):
        multiply((2 * n + OWN - 1) & (OWN - 1), lhs1, rhs1)
        build(2 * n, lhs0, rhs0)
        multiply(2 * n, lhs0, rhs0)
        build(2 * n + 1, lhs1, rhs1)
        return carry

    lax.fori_loop(0, OWN // 2, two_owners, 0)

    @pl.when(phase != 0)
    def _():
        for i in (0, 1, 3, 2):
            got_block(i)
            across(i, block(i))

    multiply(OWN - 1, lhs1, rhs1)

    @pl.when(phase == 0)
    def _():
        own_tk.wait()

    for i in range(NX):
        remote(t_ref, block(i, 1 - c), kc_send.at[i], kc_recv.at[i], w, x).wait_recv()

    total = jnp.zeros((2 * PB, PB), F32)
    for ow in range(OWN):
        yy = yb[ow * AD * BB : (ow + 1) * AD * BB, :]
        hi = yy.astype(BF16)
        lo = (yy - hi.astype(F32)).astype(BF16)
        total += lax.dot_general(
            jnp.concatenate([hi, lo], axis=1), tk[ow], TN, preferred_element_type=F32
        )
    part = total[:PB] + total[PB:]
    for xx in range(NX):
        for n in range(NY * NC):
            r3[xx, n] = part[xx * 32 + n * 4 : xx * 32 + n * 4 + 4]

    waits = []
    for dx, dy in FAR_FIRST:
        for dc in (1, 0):
            d = (dx * NY + dy) * NC + dc
            if d:
                xt, yt, ct = at_x(dx), at_y(dy), c ^ dc
                copy = remote(r3.at[xt, yt * NC + ct], g1.at[d], p1_send.at[d], p1_recv.at[d], place(z, yt, ct), xt)
                copy.start()
                waits.append(copy)
    total4 = r3[x, y * NC + c]
    for copy in waits:
        copy.wait_recv()
    sends += waits
    for d in range(1, PEERS * NC):
        total4 += g1[d]
    mine[...] = total4

    waits = []
    for dz in sorted(range(1, NZ), key=lambda n: -min(n, NZ - n)):
        copy = remote(mine, g2.at[z], p2_send.at[dz], p2_recv.at[dz], place(at_z(dz), y, c), x)
        copy.start()
        waits.append(copy)
    g2[z] = total4
    for copy in sends:
        copy.wait_send()
    for i in range(NX):
        remote(t_ref, block(i), kc_send.at[i], kc_recv.at[i], w, x).wait_send()

    @pl.when(phase == 0)
    def _():
        for i in range(3):
            remote(t_ref, block(0), ka_send.at[i], k_recv.at[0], w, x).wait_send()
        for i in range(3 * NX):
            remote(t_ref, block(0), kb_send.at[i], k_recv.at[0], w, x).wait_send()
    for copy in waits:
        copy.wait_recv()
    sends = waits
    total4 = g2[0]
    for n in range(1, NZ):
        total4 += g2[n]
    fin[...] = total4

    waits = []
    here = y * NC + c
    for n in (4, 5, 2, 3, 6, 7, 1):
        dy, dc = n // NC, n % NC
        copy = remote(
            fin, g3.at[here], p3_send.at[n], p3_recv.at[n], place(z, at_y(dy), c ^ dc), x
        )
        copy.start()
        waits.append(copy)
    g3[here] = total4
    for copy in sends:
        copy.wait_send()
    for copy in waits:
        copy.wait_recv()
    for n in range(NY * NC):
        out_ref[n * 4 : (n + 1) * 4, :] = g3[n]

    for copy in waits:
        copy.wait_send()


def local(three_center, occ_green, virt_green, occ_column, partner_live):
    t = three_center.reshape(AD, 8, 8, PB).transpose(0, 2, 1, 3).reshape(AD * BB, PB)
    occ = occ_green.transpose(0, 2, 3, 1).reshape(AD, BB, 32)
    virt = virt_green.transpose(0, 2, 3, 1).reshape(AD, BB, 32)
    vmem = pl.BlockSpec(memory_space=pltpu.VMEM)
    dma = pltpu.SemaphoreType.DMA
    return pl.pallas_call(
        kernel,
        out_shape=jax.ShapeDtypeStruct((32, PB), F32),
        in_specs=[pl.BlockSpec(memory_space=pltpu.HBM)] * 5,
        out_specs=vmem,
        scratch_shapes=[
            pltpu.VMEM((AD, BB, 32), BF16),
            pltpu.VMEM((AD, BB, 32), BF16),
            pltpu.VMEM((AD, 32), jnp.int32),
            pltpu.VMEM((AD, 32), jnp.int32),
            pltpu.VMEM((PEERS, 32, PB), BF16),
            pltpu.VMEM((PEERS, 32, PB), BF16),
            pltpu.VMEM((NY * AD * BB, PB), BF16),
            pltpu.VMEM((OWN, AD * BB, PB), BF16),
            pltpu.VMEM((PEERS, PB), jnp.int32),
            pltpu.SMEM((PEERS, PB), jnp.int32),
            pltpu.VMEM((PEERS * OWN, 8, PB), F32),
            pltpu.VMEM((PEERS * OWN, 8, PB), F32),
            pltpu.VMEM((AD * BB, PEERS * PB), BF16),
            pltpu.VMEM((AD * BB, PEERS * PB), BF16),
            pltpu.VMEM((PEERS * PB, PB), BF16),
            pltpu.VMEM((PEERS * PB, PB), BF16),
            pltpu.VMEM((OWN * AD * BB, PB), F32),
            pltpu.VMEM((NX, NY * NC, 4, PB), F32),
            pltpu.VMEM((PEERS * NC, 4, PB), F32),
            pltpu.VMEM((4, PB), F32),
            pltpu.VMEM((NZ, 4, PB), F32),
            pltpu.VMEM((4, PB), F32),
            pltpu.VMEM((NY * NC, 4, PB), F32),
            dma((PEERS,)), dma((PEERS,)),
            dma((NY,)), dma((NY,)),
            dma((NX,)), dma((3 * NX,)), dma((NX,)), dma((NX,)), dma((NX,)),
            dma((PEERS * NC,)), dma((PEERS * NC,)),
            dma((NZ,)), dma((NZ,)),
            dma((NY * NC,)), dma((NY * NC,)),
            dma((8,)),
        ],
        compiler_params=pltpu.CompilerParams(
            collective_id=0, has_side_effects=True, vmem_limit_bytes=32 * 1024 * 1024
        ),
    )(*[pltpu.with_memory_space_constraint(v, pltpu.HBM) for v in (t, occ, virt, occ_column, partner_live)])


def solution(mesh):
    placed = (
        P("wide", None, None),
        P("wide", "pair", None, None),
        P("wide", "pair", None, None),
        P("wide", "pair"),
        P("wide", "pair"),
    )
    return jax.shard_map(
        local, mesh=mesh, in_specs=placed, out_specs=P("pair", None), check_vma=False
    )
```

```python
import jax
import jax.numpy as jnp
from jax import lax
from jax.experimental import pallas as pl
from jax.experimental.pallas import tpu as pltpu
from jax.sharding import PartitionSpec as P

NZ, NY, NC, NX = 16, 4, 2, 4
PEERS = NX * NY
OWN = 8
CAP = 2
AD = 4
BB = 64
PB = 128
MESH = pl.DeviceIdType.MESH
F32 = jnp.float32
FAR_FIRST = sorted(
    ((dx, dy) for dx in range(NX) for dy in range(NY)), key=lambda o: -min(o[0], NX - o[0]) - min(o[1], NY - o[1])
)
BF16 = jnp.bfloat16
NT = (((1,), (1,)), ((), ()))
TN = (((0,), (0,)), ((), ()))


def iota(shape, dim):
    return lax.broadcasted_iota(jnp.int32, shape, dim)


def one_hot(cond):
    return jnp.where(cond, 1.0, 0.0)


def kernel(
    t_hbm, occ_hbm, virt_hbm, col_hbm, live_hbm, out_ref,
    occ_ref, virt_ref, col_ref, live_ref, sbuf, rbuf, ta, tk, meta_v, meta_s, oo, vv, lhs0, lhs1, rhs0, rhs1, yb, r3, g1, mine, g2, fin, g3,
    u_send, u_recv, a_send, a_recv, ka_send, kb_send, kc_send, k_recv, kc_recv,
    p1_send, p1_recv, p2_send, p2_recv, p3_send, p3_recv, loc,
):
    w = lax.axis_index("wide")
    x = lax.axis_index("pair")
    z = w >> 3
    y = (w >> 1) & 3
    c = w & 1

    def at_x(n):
        return (x + n) & (NX - 1)

    def at_y(n):
        return (y + n) & (NY - 1)

    def at_z(n):
        return (z + NZ + n) & (NZ - 1)

    def place(zz, yy, cc):
        return zz * (NY * NC) + yy * NC + cc

    def remote(src, dst, ss, rs, wide, pair):
        return pltpu.make_async_remote_copy(
            src_ref=src, dst_ref=dst, send_sem=ss, recv_sem=rs, device_id=(wide, pair), device_id_type=MESH
        )

    t_ref = ta.at[pl.ds(0, AD * BB)]
    load_t = pltpu.make_async_copy(t_hbm, t_ref, loc.at[0])
    loads = [
        pltpu.make_async_copy(src, dst, loc.at[4 + n])
        for n, (src, dst) in enumerate(
            ((col_hbm, col_ref), (live_hbm, live_ref), (occ_hbm, occ_ref), (virt_hbm, virt_ref))
        )
    ]
    for copy in loads:
        copy.start()
    load_t.start()

    greeted = [(at_z(dz), y, c, x) for dz in (NX, -NX)]
    greeted += [(z, at_y(dy), c, at_x(dx)) for dx, dy in FAR_FIRST if dx + dy]
    greeted += [(at_z(dz), y, c, x) for dz in (3, -3, 2, -2, 1, -1)]
    greeted += [(z, y, 1 - c, x)]
    barrier = pltpu.get_barrier_semaphore()
    for zz, yy, cc, xx in greeted:
        pl.semaphore_signal(barrier, inc=1, device_id=(place(zz, yy, cc), xx), device_id_type=MESH)
    load_t.wait()
    pl.semaphore_wait(barrier, len(greeted))
    sends = []

    phase = (z + NZ - x) & (NX - 1)
    qs = at_z(-phase) >> 2

    def block(i, core=c):
        return tk.at[((qs + NX - i) & (NX - 1)) * NC + core]

    def got_block(i):
        remote(t_ref, block(i), ka_send.at[0], k_recv.at[i], w, x).wait_recv()

    def to_z(src, dst, ss, rs, dz):
        remote(src, dst, ss, rs, place(at_z(dz), y, c), x).start()

    def beside(src, dst, first, i, side):
        for n in range(3):
            to_z(src, dst, kb_send.at[first + n], k_recv.at[i], side * (n + 1))

    def across(i, src):
        remote(src, block(i), kc_send.at[i], kc_recv.at[i], place(z, y, 1 - c), x).start()

    own_tk = pltpu.make_async_copy(t_ref, block(0), loc.at[2])

    @pl.when(phase == 0)
    def _():
        to_z(t_ref, block(0), ka_send.at[0], k_recv.at[1], NX)
        to_z(t_ref, block(0), ka_send.at[1], k_recv.at[3], -NX)
        beside(t_ref, block(0), 0, 0, 1)
        beside(t_ref, block(0), 3, 3, -1)
        across(0, t_ref)
        own_tk.start()

    for copy in loads:
        copy.wait()

    tri = one_hot(iota((32, 32), 0) < iota((32, 32), 1)).astype(BF16)
    base = jnp.zeros((PEERS * OWN, 1), F32)
    packed = jnp.zeros((PEERS * OWN * CAP, PB), F32)
    codes = jnp.zeros((PEERS, PB), F32)
    for a in range(AD):
        k = col_ref[a : a + 1, :]
        owner = k // AD
        zk, yk, ck = owner // (NY * NC), (owner // NC) % NY, owner % NC
        dest = (zk % NX) * NY + yk
        ow = (zk // NX) * NC + ck
        hit = one_hot(iota((PEERS * OWN, 32), 0) == dest * OWN + ow)
        hit16 = hit.astype(BF16)
        before = jnp.dot(hit16, tri, preferred_element_type=F32) + base
        base = base + jnp.sum(hit, axis=1, keepdims=True)
        rank = jnp.sum(hit * before, axis=0, keepdims=True).astype(jnp.int32)
        inner = rank * OWN + ow
        take = (iota((PEERS * OWN * CAP, 32), 0) == dest * (OWN * CAP) + inner) & (live_ref[a : a + 1, :] > 0)
        units = jnp.concatenate([occ_ref[a], virt_ref[a]], axis=0)
        packed += lax.dot_general(one_hot(take).astype(BF16), units, NT, preferred_element_type=F32)
        code = jnp.where(iota((PEERS, 32), 0) == dest, (a * AD + k % AD).astype(F32), 0.0).astype(BF16)
        spot = one_hot(iota((PB, 32), 0) == inner).astype(BF16)
        codes += lax.dot_general(code, spot, NT, preferred_element_type=F32)
    for j in range(PEERS):
        sbuf[j, 0:16, :] = packed[j * 16 : (j + 1) * 16].astype(BF16)
        sbuf[j, 16:32, :] = jnp.broadcast_to(codes[j : j + 1], (16, PB)).astype(BF16)

    offsets = [(dx, dy) for dx in range(NX) for dy in range(NY)]
    for dx, dy in FAR_FIRST:
        d = dx * NY + dy
        if d:
            xt, yt = at_x(dx), at_y(dy)
            copy = remote(sbuf.at[xt * NY + yt], rbuf.at[d], u_send.at[d], u_recv.at[d], place(z, yt, c), xt)
            copy.start()
            sends.append(copy)
    own_units = pltpu.make_async_copy(sbuf.at[x * NY + y], rbuf.at[0], loc.at[1])
    own_units.start()

    arrivals = []
    for dy in (2, 1, 3):
        copy = remote(
            t_ref, ta.at[pl.ds(dy * AD * BB, AD * BB)], a_send.at[dy], a_recv.at[dy], place(z, at_y(dy), c), x
        )
        copy.start()
        arrivals.append(copy)
        sends.append(copy)

    @pl.when(phase == 0)
    def _():
        got_block(1)

        @pl.when(c == 0)
        def _():
            to_z(block(1), block(1), ka_send.at[2], k_recv.at[2], NX)

        beside(block(1), block(1), 6, 1, 1)
        across(1, block(1))
        got_block(3)

        @pl.when(c == 1)
        def _():
            to_z(block(3), block(3), ka_send.at[2], k_recv.at[2], -NX)

        beside(block(3), block(3), 9, 2, -1)
        across(3, block(3))

    own_units.wait()
    for d in range(1, PEERS):
        remote(sbuf.at[0], rbuf.at[d], u_send.at[d], u_recv.at[d], w, x).wait_recv()
    for d in range(PEERS):
        meta_v[d : d + 1, :] = rbuf[d, 16:17, :].astype(F32).astype(jnp.int32)
    to_smem = pltpu.make_async_copy(meta_v, meta_s, loc.at[3])
    to_smem.start()
    got = rbuf[:, 0:16, :].astype(F32).reshape(PEERS, CAP, OWN, PB)
    both = jnp.concatenate(
        [got[:, 0].reshape(PEERS * OWN, PB).astype(BF16), got[:, 1].reshape(PEERS * OWN, PB).astype(BF16)], axis=1
    )
    row = iota((CAP * PB, PB), 0)
    lane = iota((CAP * PB, PB), 1)
    for f, arr in enumerate((oo, vv)):
        pick = (lane % 8) if f == 0 else (lane // 8) % 8
        target = (lane // BB) * PB + f * BB + pick * 8
        for g in range(8):
            sel = one_hot(row == target + g).astype(BF16)
            arr[:, g, :] = jnp.dot(both, sel, preferred_element_type=F32)
    to_smem.wait()

    for copy in arrivals:
        copy.wait_recv()

    def build(ow, lhs, rhs):
        low = iota((8, PB), 1) < BB
        for dy in range(NY):
            atoms = [ta[(dy * AD + a) * BB : (dy * AD + a + 1) * BB, :] for a in range(AD)]
            for dx in range(NX):
                d = dx * NY + dy
                c0, c1 = meta_s[d, ow], meta_s[d, OWN + ow]
                kv = jnp.where(low, c0 & 3, c1 & 3)
                o = oo[d * OWN + ow]
                v = vv[d * OWN + ow]
                wide_v = [
                    jnp.concatenate([jnp.broadcast_to(v[s + n : s + n + 1, :], (8, PB)) for n in range(2)], axis=0)
                    for s in range(0, 8, 2)
                ]
                wide_v = [t.astype(BF16) for t in wide_v]
                for kk in range(AD):
                    ok = jnp.where(kv == kk, o, 0.0)
                    ok = jnp.concatenate([ok, ok], axis=0).astype(BF16)
                    for n, t in enumerate(wide_v):
                        lhs[kk * BB + n * 16 : kk * BB + n * 16 + 16, d * PB : (d + 1) * PB] = ok * t
                for cap, code in ((0, c0), (1, c1)):
                    low_pair = jnp.where((code & 4) == 0, atoms[0], atoms[1])
                    high_pair = jnp.where((code & 4) == 0, atoms[2], atoms[3])
                    rhs[d * PB + cap * BB : d * PB + (cap + 1) * BB, :] = jnp.where(
                        (code & 8) == 0, low_pair, high_pair
                    )

    def multiply(ow, lhs, rhs):
        yb[pl.ds(pl.multiple_of(ow * AD * BB, AD * BB), AD * BB), :] = jnp.dot(
            lhs[...], rhs[...], preferred_element_type=F32
        )

    def two_owners(n, carry):
        multiply((2 * n + OWN - 1) & (OWN - 1), lhs1, rhs1)
        build(2 * n, lhs0, rhs0)
        multiply(2 * n, lhs0, rhs0)
        build(2 * n + 1, lhs1, rhs1)
        return carry

    lax.fori_loop(0, OWN // 2, two_owners, 0)

    @pl.when(phase != 0)
    def _():
        for i in (0, 3, 1):
            got_block(i)
            across(i, block(i))

    got_block(2)
    across(2, block(2))

    multiply(OWN - 1, lhs1, rhs1)

    @pl.when(phase == 0)
    def _():
        own_tk.wait()

    for i in range(NX):
        remote(t_ref, block(i, 1 - c), kc_send.at[i], kc_recv.at[i], w, x).wait_recv()

    total = jnp.zeros((2 * PB, PB), F32)
    for ow in range(OWN):
        yy = yb[ow * AD * BB : (ow + 1) * AD * BB, :]
        hi = yy.astype(BF16)
        lo = (yy - hi.astype(F32)).astype(BF16)
        total += lax.dot_general(
            jnp.concatenate([hi, lo], axis=1), tk[ow], TN, preferred_element_type=F32
        )
    part = total[:PB] + total[PB:]
    for xx in range(NX):
        for n in range(NY * NC):
            r3[xx, n] = part[xx * 32 + n * 4 : xx * 32 + n * 4 + 4]

    waits = []
    for dx, dy in FAR_FIRST:
        for dc in (1, 0):
            d = (dx * NY + dy) * NC + dc
            if d:
                xt, yt, ct = at_x(dx), at_y(dy), c ^ dc
                copy = remote(r3.at[xt, yt * NC + ct], g1.at[d], p1_send.at[d], p1_recv.at[d], place(z, yt, ct), xt)
                copy.start()
                waits.append(copy)
    total4 = r3[x, y * NC + c]
    for copy in waits:
        copy.wait_recv()
    sends += waits
    for d in range(1, PEERS * NC):
        total4 += g1[d]
    mine[...] = total4

    waits = []
    for dz in sorted(range(1, NZ), key=lambda n: -min(n, NZ - n)):
        copy = remote(mine, g2.at[z], p2_send.at[dz], p2_recv.at[dz], place(at_z(dz), y, c), x)
        copy.start()
        waits.append(copy)
    g2[z] = total4
    for copy in sends:
        copy.wait_send()
    for i in range(NX):
        remote(t_ref, block(i), kc_send.at[i], kc_recv.at[i], w, x).wait_send()

    @pl.when(phase == 0)
    def _():
        for i in range(3):
            remote(t_ref, block(0), ka_send.at[i], k_recv.at[0], w, x).wait_send()
        for i in range(3 * NX):
            remote(t_ref, block(0), kb_send.at[i], k_recv.at[0], w, x).wait_send()
    for copy in waits:
        copy.wait_recv()
    sends = waits
    total4 = g2[0]
    for n in range(1, NZ):
        total4 += g2[n]
    fin[...] = total4

    waits = []
    here = y * NC + c
    for n in (4, 5, 2, 3, 6, 7, 1):
        dy, dc = n // NC, n % NC
        copy = remote(
            fin, g3.at[here], p3_send.at[n], p3_recv.at[n], place(z, at_y(dy), c ^ dc), x
        )
        copy.start()
        waits.append(copy)
    g3[here] = total4
    for copy in sends:
        copy.wait_send()
    for copy in waits:
        copy.wait_recv()
    for n in range(NY * NC):
        out_ref[n * 4 : (n + 1) * 4, :] = g3[n]

    for copy in waits:
        copy.wait_send()


def local(three_center, occ_green, virt_green, occ_column, partner_live):
    t = three_center.reshape(AD, 8, 8, PB).transpose(0, 2, 1, 3).reshape(AD * BB, PB)
    occ = occ_green.transpose(0, 2, 3, 1).reshape(AD, BB, 32)
    virt = virt_green.transpose(0, 2, 3, 1).reshape(AD, BB, 32)
    vmem = pl.BlockSpec(memory_space=pltpu.VMEM)
    dma = pltpu.SemaphoreType.DMA
    return pl.pallas_call(
        kernel,
        out_shape=jax.ShapeDtypeStruct((32, PB), F32),
        in_specs=[pl.BlockSpec(memory_space=pltpu.HBM)] * 5,
        out_specs=vmem,
        scratch_shapes=[
            pltpu.VMEM((AD, BB, 32), BF16),
            pltpu.VMEM((AD, BB, 32), BF16),
            pltpu.VMEM((AD, 32), jnp.int32),
            pltpu.VMEM((AD, 32), jnp.int32),
            pltpu.VMEM((PEERS, 32, PB), BF16),
            pltpu.VMEM((PEERS, 32, PB), BF16),
            pltpu.VMEM((NY * AD * BB, PB), BF16),
            pltpu.VMEM((OWN, AD * BB, PB), BF16),
            pltpu.VMEM((PEERS, PB), jnp.int32),
            pltpu.SMEM((PEERS, PB), jnp.int32),
            pltpu.VMEM((PEERS * OWN, 8, PB), F32),
            pltpu.VMEM((PEERS * OWN, 8, PB), F32),
            pltpu.VMEM((AD * BB, PEERS * PB), BF16),
            pltpu.VMEM((AD * BB, PEERS * PB), BF16),
            pltpu.VMEM((PEERS * PB, PB), BF16),
            pltpu.VMEM((PEERS * PB, PB), BF16),
            pltpu.VMEM((OWN * AD * BB, PB), F32),
            pltpu.VMEM((NX, NY * NC, 4, PB), F32),
            pltpu.VMEM((PEERS * NC, 4, PB), F32),
            pltpu.VMEM((4, PB), F32),
            pltpu.VMEM((NZ, 4, PB), F32),
            pltpu.VMEM((4, PB), F32),
            pltpu.VMEM((NY * NC, 4, PB), F32),
            dma((PEERS,)), dma((PEERS,)),
            dma((NY,)), dma((NY,)),
            dma((NX,)), dma((3 * NX,)), dma((NX,)), dma((NX,)), dma((NX,)),
            dma((PEERS * NC,)), dma((PEERS * NC,)),
            dma((NZ,)), dma((NZ,)),
            dma((NY * NC,)), dma((NY * NC,)),
            dma((8,)),
        ],
        compiler_params=pltpu.CompilerParams(
            collective_id=0, has_side_effects=True, vmem_limit_bytes=32 * 1024 * 1024
        ),
    )(*[pltpu.with_memory_space_constraint(v, pltpu.HBM) for v in (t, occ, virt, occ_column, partner_live)])


def solution(mesh):
    placed = (
        P("wide", None, None),
        P("wide", "pair", None, None),
        P("wide", "pair", None, None),
        P("wide", "pair"),
        P("wide", "pair"),
    )
    return jax.shard_map(
        local, mesh=mesh, in_specs=placed, out_specs=P("pair", None), check_vma=False
    )
```

```python
import jax
import jax.numpy as jnp
from jax import lax
from jax.experimental import pallas as pl
from jax.experimental.pallas import tpu as pltpu
from jax.sharding import PartitionSpec as P

NZ, NY, NC, NX = 16, 4, 2, 4
PEERS = NX * NY
OWN = 8
CAP = 2
AD = 4
BB = 64
PB = 128
MESH = pl.DeviceIdType.MESH
F32 = jnp.float32
FAR_FIRST = sorted(
    ((dx, dy) for dx in range(NX) for dy in range(NY)), key=lambda o: -min(o[0], NX - o[0]) - min(o[1], NY - o[1])
)
BF16 = jnp.bfloat16
NT = (((1,), (1,)), ((), ()))
TN = (((0,), (0,)), ((), ()))


def iota(shape, dim):
    return lax.broadcasted_iota(jnp.int32, shape, dim)


def one_hot(cond):
    return jnp.where(cond, 1.0, 0.0)


def kernel(
    t_hbm, occ_hbm, virt_hbm, col_hbm, live_hbm, out_ref,
    occ_ref, virt_ref, col_ref, live_ref, sbuf, rbuf, ta, tk, meta_v, meta_s, oo, vv, lhs0, lhs1, rhs0, rhs1, yb, r3, g1, mine, g2, fin, g3,
    u_send, u_recv, a_send, a_recv, ka_send, kb_send, kc_send, k_recv, kc_recv,
    p1_send, p1_recv, p2_send, p2_recv, p3_send, p3_recv, loc,
):
    w = lax.axis_index("wide")
    x = lax.axis_index("pair")
    z = w >> 3
    y = (w >> 1) & 3
    c = w & 1

    def at_x(n):
        return (x + n) & (NX - 1)

    def at_y(n):
        return (y + n) & (NY - 1)

    def at_z(n):
        return (z + NZ + n) & (NZ - 1)

    def place(zz, yy, cc):
        return zz * (NY * NC) + yy * NC + cc

    def remote(src, dst, ss, rs, wide, pair):
        return pltpu.make_async_remote_copy(
            src_ref=src, dst_ref=dst, send_sem=ss, recv_sem=rs, device_id=(wide, pair), device_id_type=MESH
        )

    t_ref = ta.at[pl.ds(0, AD * BB)]
    load_t = pltpu.make_async_copy(t_hbm, t_ref, loc.at[0])
    loads = [
        pltpu.make_async_copy(src, dst, loc.at[4 + n])
        for n, (src, dst) in enumerate(
            ((col_hbm, col_ref), (live_hbm, live_ref), (occ_hbm, occ_ref), (virt_hbm, virt_ref))
        )
    ]
    for copy in loads:
        copy.start()
    load_t.start()

    greeted = [(at_z(dz), y, c, x) for dz in (NX, -NX)]
    greeted += [(z, at_y(dy), c, at_x(dx)) for dx, dy in FAR_FIRST if dx + dy]
    greeted += [(at_z(dz), y, c, x) for dz in (3, -3, 2, -2, 1, -1)]
    greeted += [(z, y, 1 - c, x)]
    barrier = pltpu.get_barrier_semaphore()
    for zz, yy, cc, xx in greeted:
        pl.semaphore_signal(barrier, inc=1, device_id=(place(zz, yy, cc), xx), device_id_type=MESH)
    load_t.wait()
    pl.semaphore_wait(barrier, len(greeted))
    sends = []

    phase = (z + NZ - x) & (NX - 1)
    qs = at_z(-phase) >> 2

    def block(i, core=c):
        return tk.at[((qs + NX - i) & (NX - 1)) * NC + core]

    def got_block(i):
        remote(t_ref, block(i), ka_send.at[0], k_recv.at[i], w, x).wait_recv()

    def to_z(src, dst, ss, rs, dz):
        remote(src, dst, ss, rs, place(at_z(dz), y, c), x).start()

    def beside(src, dst, first, i, side):
        for n in (2, 1, 0):
            to_z(src, dst, kb_send.at[first + n], k_recv.at[i], side * (n + 1))

    def across(i, src):
        remote(src, block(i), kc_send.at[i], kc_recv.at[i], place(z, y, 1 - c), x).start()

    own_tk = pltpu.make_async_copy(t_ref, block(0), loc.at[2])

    @pl.when(phase == 0)
    def _():
        to_z(t_ref, block(0), ka_send.at[0], k_recv.at[1], NX)
        to_z(t_ref, block(0), ka_send.at[1], k_recv.at[3], -NX)
        beside(t_ref, block(0), 0, 0, 1)
        beside(t_ref, block(0), 3, 3, -1)
        across(0, t_ref)
        own_tk.start()

    for copy in loads:
        copy.wait()

    tri = one_hot(iota((32, 32), 0) < iota((32, 32), 1)).astype(BF16)
    base = jnp.zeros((PEERS * OWN, 1), F32)
    packed = jnp.zeros((PEERS * OWN * CAP, PB), F32)
    codes = jnp.zeros((PEERS, PB), F32)
    for a in range(AD):
        k = col_ref[a : a + 1, :]
        owner = k // AD
        zk, yk, ck = owner // (NY * NC), (owner // NC) % NY, owner % NC
        dest = (zk % NX) * NY + yk
        ow = (zk // NX) * NC + ck
        hit = one_hot(iota((PEERS * OWN, 32), 0) == dest * OWN + ow)
        hit16 = hit.astype(BF16)
        before = jnp.dot(hit16, tri, preferred_element_type=F32) + base
        base = base + jnp.sum(hit, axis=1, keepdims=True)
        rank = jnp.sum(hit * before, axis=0, keepdims=True).astype(jnp.int32)
        inner = rank * OWN + ow
        take = (iota((PEERS * OWN * CAP, 32), 0) == dest * (OWN * CAP) + inner) & (live_ref[a : a + 1, :] > 0)
        units = jnp.concatenate([occ_ref[a], virt_ref[a]], axis=0)
        packed += lax.dot_general(one_hot(take).astype(BF16), units, NT, preferred_element_type=F32)
        code = jnp.where(iota((PEERS, 32), 0) == dest, (a * AD + k % AD).astype(F32), 0.0).astype(BF16)
        spot = one_hot(iota((PB, 32), 0) == inner).astype(BF16)
        codes += lax.dot_general(code, spot, NT, preferred_element_type=F32)
    for j in range(PEERS):
        sbuf[j, 0:16, :] = packed[j * 16 : (j + 1) * 16].astype(BF16)
        sbuf[j, 16:32, :] = jnp.broadcast_to(codes[j : j + 1], (16, PB)).astype(BF16)

    offsets = [(dx, dy) for dx in range(NX) for dy in range(NY)]
    for dx, dy in FAR_FIRST:
        d = dx * NY + dy
        if d:
            xt, yt = at_x(dx), at_y(dy)
            copy = remote(sbuf.at[xt * NY + yt], rbuf.at[d], u_send.at[d], u_recv.at[d], place(z, yt, c), xt)
            copy.start()
            sends.append(copy)
    own_units = pltpu.make_async_copy(sbuf.at[x * NY + y], rbuf.at[0], loc.at[1])
    own_units.start()

    arrivals = []
    for dy in (2, 1, 3):
        copy = remote(
            t_ref, ta.at[pl.ds(dy * AD * BB, AD * BB)], a_send.at[dy], a_recv.at[dy], place(z, at_y(dy), c), x
        )
        copy.start()
        arrivals.append(copy)
        sends.append(copy)

    @pl.when(phase == 0)
    def _():
        got_block(1)

        @pl.when(c == 0)
        def _():
            to_z(block(1), block(1), ka_send.at[2], k_recv.at[2], NX)

        beside(block(1), block(1), 6, 1, 1)
        across(1, block(1))
        got_block(3)

        @pl.when(c == 1)
        def _():
            to_z(block(3), block(3), ka_send.at[2], k_recv.at[2], -NX)

        beside(block(3), block(3), 9, 2, -1)
        across(3, block(3))

    own_units.wait()
    for d in range(1, PEERS):
        remote(sbuf.at[0], rbuf.at[d], u_send.at[d], u_recv.at[d], w, x).wait_recv()
    for d in range(PEERS):
        meta_v[d : d + 1, :] = rbuf[d, 16:17, :].astype(F32).astype(jnp.int32)
    to_smem = pltpu.make_async_copy(meta_v, meta_s, loc.at[3])
    to_smem.start()
    got = rbuf[:, 0:16, :].astype(F32).reshape(PEERS, CAP, OWN, PB)
    both = jnp.concatenate(
        [got[:, 0].reshape(PEERS * OWN, PB).astype(BF16), got[:, 1].reshape(PEERS * OWN, PB).astype(BF16)], axis=1
    )
    row = iota((CAP * PB, PB), 0)
    lane = iota((CAP * PB, PB), 1)
    for f, arr in enumerate((oo, vv)):
        pick = (lane % 8) if f == 0 else (lane // 8) % 8
        target = (lane // BB) * PB + f * BB + pick * 8
        for g in range(8):
            sel = one_hot(row == target + g).astype(BF16)
            arr[:, g, :] = jnp.dot(both, sel, preferred_element_type=F32)
    to_smem.wait()

    for copy in arrivals:
        copy.wait_recv()

    def build(ow, lhs, rhs, d):
        low = iota((8, PB), 1) < BB
        dy = d % NY
        c0, c1 = meta_s[d, ow], meta_s[d, OWN + ow]
        kv = jnp.where(low, c0 & 3, c1 & 3)
        o = oo[d * OWN + ow]
        v = vv[d * OWN + ow]
        wide_v = [
            jnp.concatenate([jnp.broadcast_to(v[s + n : s + n + 1, :], (8, PB)) for n in range(2)], axis=0)
            for s in range(0, 8, 2)
        ]
        wide_v = [t.astype(BF16) for t in wide_v]
        for kk in range(AD):
            ok = jnp.where(kv == kk, o, 0.0)
            ok = jnp.concatenate([ok, ok], axis=0).astype(BF16)
            for n, t in enumerate(wide_v):
                lhs[kk * BB + n * 16 : kk * BB + n * 16 + 16, d * PB : (d + 1) * PB] = ok * t
        atoms = [ta[(dy * AD + a) * BB : (dy * AD + a + 1) * BB, :] for a in range(AD)]
        for cap, code in ((0, c0), (1, c1)):
            low_pair = jnp.where((code & 4) == 0, atoms[0], atoms[1])
            high_pair = jnp.where((code & 4) == 0, atoms[2], atoms[3])
            rhs[d * PB + cap * BB : d * PB + (cap + 1) * BB, :] = jnp.where((code & 8) == 0, low_pair, high_pair)

    def multiply_and_build(done, lhs_done, rhs_done, ow, lhs, rhs):
        total = jnp.zeros((AD * BB, PB), F32)
        for d in range(0, PEERS, 2):
            span = slice(d * PB, (d + 2) * PB)
            total += jnp.dot(lhs_done[:, span], rhs_done[span, :], preferred_element_type=F32)
            if ow is not None:
                for n in range(2):
                    build(ow, lhs, rhs, d + n)
        yb[pl.ds(pl.multiple_of(done * AD * BB, AD * BB), AD * BB), :] = total

    def two_owners(n, carry):
        multiply_and_build((2 * n + OWN - 1) & (OWN - 1), lhs1, rhs1, 2 * n, lhs0, rhs0)
        multiply_and_build(2 * n, lhs0, rhs0, 2 * n + 1, lhs1, rhs1)
        return carry

    lax.fori_loop(0, OWN // 2, two_owners, 0)

    @pl.when(phase != 0)
    def _():
        for i in (0, 3, 1):
            got_block(i)
            across(i, block(i))

    got_block(2)
    across(2, block(2))

    multiply_and_build(OWN - 1, lhs1, rhs1, None, None, None)

    @pl.when(phase == 0)
    def _():
        own_tk.wait()

    for i in range(NX):
        remote(t_ref, block(i, 1 - c), kc_send.at[i], kc_recv.at[i], w, x).wait_recv()

    total = jnp.zeros((2 * PB, PB), F32)
    for ow in range(OWN):
        yy = yb[ow * AD * BB : (ow + 1) * AD * BB, :]
        hi = yy.astype(BF16)
        lo = (yy - hi.astype(F32)).astype(BF16)
        total += lax.dot_general(
            jnp.concatenate([hi, lo], axis=1), tk[ow], TN, preferred_element_type=F32
        )
    part = total[:PB] + total[PB:]
    for xx in range(NX):
        for n in range(NY * NC):
            r3[xx, n] = part[xx * 32 + n * 4 : xx * 32 + n * 4 + 4]

    waits = []
    for dx, dy in FAR_FIRST:
        for dc in (1, 0):
            d = (dx * NY + dy) * NC + dc
            if d:
                xt, yt, ct = at_x(dx), at_y(dy), c ^ dc
                copy = remote(r3.at[xt, yt * NC + ct], g1.at[d], p1_send.at[d], p1_recv.at[d], place(z, yt, ct), xt)
                copy.start()
                waits.append(copy)
    total4 = r3[x, y * NC + c]
    for copy in waits:
        copy.wait_recv()
    sends += waits
    for d in range(1, PEERS * NC):
        total4 += g1[d]
    mine[...] = total4

    waits = []
    for dz in sorted(range(1, NZ), key=lambda n: -min(n, NZ - n)):
        copy = remote(mine, g2.at[z], p2_send.at[dz], p2_recv.at[dz], place(at_z(dz), y, c), x)
        copy.start()
        waits.append(copy)
    g2[z] = total4
    for copy in sends:
        copy.wait_send()
    for i in range(NX):
        remote(t_ref, block(i), kc_send.at[i], kc_recv.at[i], w, x).wait_send()

    @pl.when(phase == 0)
    def _():
        for i in range(3):
            remote(t_ref, block(0), ka_send.at[i], k_recv.at[0], w, x).wait_send()
        for i in range(3 * NX):
            remote(t_ref, block(0), kb_send.at[i], k_recv.at[0], w, x).wait_send()
    for copy in waits:
        copy.wait_recv()
    sends = waits
    total4 = g2[0]
    for n in range(1, NZ):
        total4 += g2[n]
    fin[...] = total4

    waits = []
    here = y * NC + c
    for n in (4, 5, 2, 3, 6, 7, 1):
        dy, dc = n // NC, n % NC
        copy = remote(
            fin, g3.at[here], p3_send.at[n], p3_recv.at[n], place(z, at_y(dy), c ^ dc), x
        )
        copy.start()
        waits.append(copy)
    g3[here] = total4
    for copy in sends:
        copy.wait_send()
    for copy in waits:
        copy.wait_recv()
    for n in range(NY * NC):
        out_ref[n * 4 : (n + 1) * 4, :] = g3[n]

    for copy in waits:
        copy.wait_send()


def local(three_center, occ_green, virt_green, occ_column, partner_live):
    t = three_center.reshape(AD, 8, 8, PB).transpose(0, 2, 1, 3).reshape(AD * BB, PB)
    occ = occ_green.transpose(0, 2, 3, 1).reshape(AD, BB, 32)
    virt = virt_green.transpose(0, 2, 3, 1).reshape(AD, BB, 32)
    vmem = pl.BlockSpec(memory_space=pltpu.VMEM)
    dma = pltpu.SemaphoreType.DMA
    return pl.pallas_call(
        kernel,
        out_shape=jax.ShapeDtypeStruct((32, PB), F32),
        in_specs=[pl.BlockSpec(memory_space=pltpu.HBM)] * 5,
        out_specs=vmem,
        scratch_shapes=[
            pltpu.VMEM((AD, BB, 32), BF16),
            pltpu.VMEM((AD, BB, 32), BF16),
            pltpu.VMEM((AD, 32), jnp.int32),
            pltpu.VMEM((AD, 32), jnp.int32),
            pltpu.VMEM((PEERS, 32, PB), BF16),
            pltpu.VMEM((PEERS, 32, PB), BF16),
            pltpu.VMEM((NY * AD * BB, PB), BF16),
            pltpu.VMEM((OWN, AD * BB, PB), BF16),
            pltpu.VMEM((PEERS, PB), jnp.int32),
            pltpu.SMEM((PEERS, PB), jnp.int32),
            pltpu.VMEM((PEERS * OWN, 8, PB), F32),
            pltpu.VMEM((PEERS * OWN, 8, PB), F32),
            pltpu.VMEM((AD * BB, PEERS * PB), BF16),
            pltpu.VMEM((AD * BB, PEERS * PB), BF16),
            pltpu.VMEM((PEERS * PB, PB), BF16),
            pltpu.VMEM((PEERS * PB, PB), BF16),
            pltpu.VMEM((OWN * AD * BB, PB), F32),
            pltpu.VMEM((NX, NY * NC, 4, PB), F32),
            pltpu.VMEM((PEERS * NC, 4, PB), F32),
            pltpu.VMEM((4, PB), F32),
            pltpu.VMEM((NZ, 4, PB), F32),
            pltpu.VMEM((4, PB), F32),
            pltpu.VMEM((NY * NC, 4, PB), F32),
            dma((PEERS,)), dma((PEERS,)),
            dma((NY,)), dma((NY,)),
            dma((NX,)), dma((3 * NX,)), dma((NX,)), dma((NX,)), dma((NX,)),
            dma((PEERS * NC,)), dma((PEERS * NC,)),
            dma((NZ,)), dma((NZ,)),
            dma((NY * NC,)), dma((NY * NC,)),
            dma((8,)),
        ],
        compiler_params=pltpu.CompilerParams(
            collective_id=0, has_side_effects=True, vmem_limit_bytes=32 * 1024 * 1024
        ),
    )(*[pltpu.with_memory_space_constraint(v, pltpu.HBM) for v in (t, occ, virt, occ_column, partner_live)])


def solution(mesh):
    placed = (
        P("wide", None, None),
        P("wide", "pair", None, None),
        P("wide", "pair", None, None),
        P("wide", "pair"),
        P("wide", "pair"),
    )
    return jax.shard_map(
        local, mesh=mesh, in_specs=placed, out_specs=P("pair", None), check_vma=False
    )
```

```python
import jax
import jax.numpy as jnp
from jax import lax
from jax.experimental import pallas as pl
from jax.experimental.pallas import tpu as pltpu
from jax.sharding import PartitionSpec as P

NZ, NY, NC, NX = 16, 4, 2, 4
PEERS = NX * NY
OWN = 8
CAP = 2
AD = 4
BB = 64
PB = 128
MESH = pl.DeviceIdType.MESH
F32 = jnp.float32
FAR_FIRST = sorted(
    ((dx, dy) for dx in range(NX) for dy in range(NY)), key=lambda o: -min(o[0], NX - o[0]) - min(o[1], NY - o[1])
)
BF16 = jnp.bfloat16
NT = (((1,), (1,)), ((), ()))
TN = (((0,), (0,)), ((), ()))


def iota(shape, dim):
    return lax.broadcasted_iota(jnp.int32, shape, dim)


def one_hot(cond):
    return jnp.where(cond, 1.0, 0.0)


def kernel(
    t_hbm, occ_hbm, virt_hbm, col_hbm, live_hbm, out_ref,
    occ_ref, virt_ref, col_ref, live_ref, sbuf, rbuf, ta, tk, meta_v, meta_s, sel, oo, vv, lhs0, lhs1, rhs0, rhs1, yb, r3, g1, mine, g2, fin, g3,
    u_send, u_recv, a_send, a_recv, ka_send, kb_send, kc_send, k_recv, kc_recv,
    p1_send, p1_recv, p2_send, p2_recv, p3_send, p3_recv, loc,
):
    w = lax.axis_index("wide")
    x = lax.axis_index("pair")
    z = w >> 3
    y = (w >> 1) & 3
    c = w & 1

    def at_x(n):
        return (x + n) & (NX - 1)

    def at_y(n):
        return (y + n) & (NY - 1)

    def at_z(n):
        return (z + NZ + n) & (NZ - 1)

    def place(zz, yy, cc):
        return zz * (NY * NC) + yy * NC + cc

    def remote(src, dst, ss, rs, wide, pair):
        return pltpu.make_async_remote_copy(
            src_ref=src, dst_ref=dst, send_sem=ss, recv_sem=rs, device_id=(wide, pair), device_id_type=MESH
        )

    t_ref = ta.at[pl.ds(0, AD * BB)]
    load_t = pltpu.make_async_copy(t_hbm, t_ref, loc.at[0])
    loads = [
        pltpu.make_async_copy(src, dst, loc.at[4 + n])
        for n, (src, dst) in enumerate(
            ((col_hbm, col_ref), (live_hbm, live_ref), (occ_hbm, occ_ref), (virt_hbm, virt_ref))
        )
    ]
    for copy in loads:
        copy.start()
    load_t.start()

    greeted = [(at_z(dz), y, c, x) for dz in (NX, -NX)]
    greeted += [(z, at_y(dy), c, at_x(dx)) for dx, dy in FAR_FIRST if dx + dy]
    greeted += [(at_z(dz), y, c, x) for dz in (3, -3, 2, -2, 1, -1)]
    greeted += [(z, y, 1 - c, x)]
    barrier = pltpu.get_barrier_semaphore()
    for zz, yy, cc, xx in greeted:
        pl.semaphore_signal(barrier, inc=1, device_id=(place(zz, yy, cc), xx), device_id_type=MESH)
    load_t.wait()
    pl.semaphore_wait(barrier, len(greeted))
    sends = []

    phase = (z + NZ - x) & (NX - 1)
    qs = at_z(-phase) >> 2

    def block(i, core=c):
        return tk.at[((qs + NX - i) & (NX - 1)) * NC + core]

    def got_block(i):
        remote(t_ref, block(i), ka_send.at[0], k_recv.at[i], w, x).wait_recv()

    def to_z(src, dst, ss, rs, dz):
        remote(src, dst, ss, rs, place(at_z(dz), y, c), x).start()

    def beside(src, dst, first, i, side):
        for n in (2, 1, 0):
            to_z(src, dst, kb_send.at[first + n], k_recv.at[i], side * (n + 1))

    def across(i, src):
        remote(src, block(i), kc_send.at[i], kc_recv.at[i], place(z, y, 1 - c), x).start()

    own_tk = pltpu.make_async_copy(t_ref, block(0), loc.at[2])

    @pl.when(phase == 0)
    def _():
        to_z(t_ref, block(0), ka_send.at[0], k_recv.at[1], NX)
        to_z(t_ref, block(0), ka_send.at[1], k_recv.at[3], -NX)
        beside(t_ref, block(0), 0, 0, 1)
        beside(t_ref, block(0), 3, 3, -1)
        across(0, t_ref)
        own_tk.start()

    for copy in loads:
        copy.wait()

    tri = one_hot(iota((32, 32), 0) < iota((32, 32), 1)).astype(BF16)
    base = jnp.zeros((PEERS * OWN, 1), F32)
    packed = jnp.zeros((PEERS * OWN * CAP, PB), F32)
    codes = jnp.zeros((PEERS, PB), F32)
    for a in range(AD):
        k = col_ref[a : a + 1, :]
        owner = k // AD
        zk, yk, ck = owner // (NY * NC), (owner // NC) % NY, owner % NC
        dest = (zk % NX) * NY + yk
        ow = (zk // NX) * NC + ck
        hit = one_hot(iota((PEERS * OWN, 32), 0) == dest * OWN + ow)
        hit16 = hit.astype(BF16)
        before = jnp.dot(hit16, tri, preferred_element_type=F32) + base
        base = base + jnp.sum(hit, axis=1, keepdims=True)
        rank = jnp.sum(hit * before, axis=0, keepdims=True).astype(jnp.int32)
        inner = rank * OWN + ow
        take = (iota((PEERS * OWN * CAP, 32), 0) == dest * (OWN * CAP) + inner) & (live_ref[a : a + 1, :] > 0)
        units = jnp.concatenate([occ_ref[a], virt_ref[a]], axis=0)
        packed += lax.dot_general(one_hot(take).astype(BF16), units, NT, preferred_element_type=F32)
        code = jnp.where(iota((PEERS, 32), 0) == dest, (a * AD + k % AD).astype(F32), 0.0).astype(BF16)
        spot = one_hot(iota((PB, 32), 0) == inner).astype(BF16)
        codes += lax.dot_general(code, spot, NT, preferred_element_type=F32)
    for j in range(PEERS):
        sbuf[j, 0:16, :] = packed[j * 16 : (j + 1) * 16].astype(BF16)
        sbuf[j, 16:32, :] = jnp.broadcast_to(codes[j : j + 1], (16, PB)).astype(BF16)

    offsets = [(dx, dy) for dx in range(NX) for dy in range(NY)]
    for dx, dy in FAR_FIRST:
        d = dx * NY + dy
        if d:
            xt, yt = at_x(dx), at_y(dy)
            copy = remote(sbuf.at[xt * NY + yt], rbuf.at[d], u_send.at[d], u_recv.at[d], place(z, yt, c), xt)
            copy.start()
            sends.append(copy)
    own_units = pltpu.make_async_copy(sbuf.at[x * NY + y], rbuf.at[0], loc.at[1])
    own_units.start()

    row = iota((CAP * PB, PB), 0)
    lane = iota((CAP * PB, PB), 1)
    for f in range(2):
        pick = (lane % 8) if f == 0 else (lane // 8) % 8
        target = (lane // BB) * PB + f * BB + pick * 8
        for g in range(8):
            sel[f * 8 + g] = one_hot(row == target + g).astype(BF16)

    arrivals = []
    for dy in (2, 1, 3):
        copy = remote(
            t_ref, ta.at[pl.ds(dy * AD * BB, AD * BB)], a_send.at[dy], a_recv.at[dy], place(z, at_y(dy), c), x
        )
        copy.start()
        arrivals.append(copy)
        sends.append(copy)

    @pl.when(phase == 0)
    def _():
        got_block(1)

        @pl.when(c == 0)
        def _():
            to_z(block(1), block(1), ka_send.at[2], k_recv.at[2], NX)

        beside(block(1), block(1), 6, 1, 1)
        across(1, block(1))
        got_block(3)

        @pl.when(c == 1)
        def _():
            to_z(block(3), block(3), ka_send.at[2], k_recv.at[2], -NX)

        beside(block(3), block(3), 9, 2, -1)
        across(3, block(3))

    own_units.wait()
    for d in range(1, PEERS):
        remote(sbuf.at[0], rbuf.at[d], u_send.at[d], u_recv.at[d], w, x).wait_recv()
    for d in range(PEERS):
        meta_v[d : d + 1, :] = rbuf[d, 16:17, :].astype(F32).astype(jnp.int32)
    to_smem = pltpu.make_async_copy(meta_v, meta_s, loc.at[3])
    to_smem.start()
    got = rbuf[:, 0:16, :].astype(F32).reshape(PEERS, CAP, OWN, PB)
    both = jnp.concatenate(
        [got[:, 0].reshape(PEERS * OWN, PB).astype(BF16), got[:, 1].reshape(PEERS * OWN, PB).astype(BF16)], axis=1
    )
    for f, arr in enumerate((oo, vv)):
        for g in range(8):
            arr[:, g, :] = jnp.dot(both, sel[f * 8 + g], preferred_element_type=F32)
    to_smem.wait()

    for copy in arrivals:
        copy.wait_recv()

    def build(ow, lhs, rhs, d):
        low = iota((8, PB), 1) < BB
        dy = d % NY
        c0, c1 = meta_s[d, ow], meta_s[d, OWN + ow]
        kv = jnp.where(low, c0 & 3, c1 & 3)
        o = oo[d * OWN + ow]
        v = vv[d * OWN + ow]
        wide_v = [
            jnp.concatenate([jnp.broadcast_to(v[s + n : s + n + 1, :], (8, PB)) for n in range(2)], axis=0)
            for s in range(0, 8, 2)
        ]
        wide_v = [t.astype(BF16) for t in wide_v]
        for kk in range(AD):
            ok = jnp.where(kv == kk, o, 0.0)
            ok = jnp.concatenate([ok, ok], axis=0).astype(BF16)
            for n, t in enumerate(wide_v):
                lhs[kk * BB + n * 16 : kk * BB + n * 16 + 16, d * PB : (d + 1) * PB] = ok * t
        atoms = [ta[(dy * AD + a) * BB : (dy * AD + a + 1) * BB, :] for a in range(AD)]
        for cap, code in ((0, c0), (1, c1)):
            low_pair = jnp.where((code & 4) == 0, atoms[0], atoms[1])
            high_pair = jnp.where((code & 4) == 0, atoms[2], atoms[3])
            rhs[d * PB + cap * BB : d * PB + (cap + 1) * BB, :] = jnp.where((code & 8) == 0, low_pair, high_pair)

    def multiply_and_build(done, lhs_done, rhs_done, ow, lhs, rhs):
        total = jnp.zeros((AD * BB, PB), F32)
        for d in range(0, PEERS, 2):
            span = slice(d * PB, (d + 2) * PB)
            total += jnp.dot(lhs_done[:, span], rhs_done[span, :], preferred_element_type=F32)
            if ow is not None:
                for n in range(2):
                    build(ow, lhs, rhs, d + n)
        yb[pl.ds(pl.multiple_of(done * AD * BB, AD * BB), AD * BB), :] = total

    def two_owners(n, carry):
        multiply_and_build((2 * n + OWN - 1) & (OWN - 1), lhs1, rhs1, 2 * n, lhs0, rhs0)
        multiply_and_build(2 * n, lhs0, rhs0, 2 * n + 1, lhs1, rhs1)
        return carry

    lax.fori_loop(0, OWN // 2, two_owners, 0)

    @pl.when(phase != 0)
    def _():
        for i in (0, 3, 1):
            got_block(i)
            across(i, block(i))

    got_block(2)
    across(2, block(2))

    multiply_and_build(OWN - 1, lhs1, rhs1, None, None, None)

    @pl.when(phase == 0)
    def _():
        own_tk.wait()

    for i in range(NX):
        remote(t_ref, block(i, 1 - c), kc_send.at[i], kc_recv.at[i], w, x).wait_recv()

    total = jnp.zeros((2 * PB, PB), F32)
    for ow in range(OWN):
        yy = yb[ow * AD * BB : (ow + 1) * AD * BB, :]
        hi = yy.astype(BF16)
        lo = (yy - hi.astype(F32)).astype(BF16)
        total += lax.dot_general(
            jnp.concatenate([hi, lo], axis=1), tk[ow], TN, preferred_element_type=F32
        )
    part = total[:PB] + total[PB:]
    for xx in range(NX):
        for n in range(NY * NC):
            r3[xx, n] = part[xx * 32 + n * 4 : xx * 32 + n * 4 + 4]

    waits = []
    for dx, dy in FAR_FIRST:
        for dc in (1, 0):
            d = (dx * NY + dy) * NC + dc
            if d:
                xt, yt, ct = at_x(dx), at_y(dy), c ^ dc
                copy = remote(r3.at[xt, yt * NC + ct], g1.at[d], p1_send.at[d], p1_recv.at[d], place(z, yt, ct), xt)
                copy.start()
                waits.append(copy)
    total4 = r3[x, y * NC + c]
    for copy in waits:
        copy.wait_recv()
    sends += waits
    for d in range(1, PEERS * NC):
        total4 += g1[d]
    mine[...] = total4

    waits = []
    for dz in sorted(range(1, NZ), key=lambda n: -min(n, NZ - n)):
        copy = remote(mine, g2.at[z], p2_send.at[dz], p2_recv.at[dz], place(at_z(dz), y, c), x)
        copy.start()
        waits.append(copy)
    g2[z] = total4
    for copy in sends:
        copy.wait_send()
    for i in range(NX):
        remote(t_ref, block(i), kc_send.at[i], kc_recv.at[i], w, x).wait_send()

    @pl.when(phase == 0)
    def _():
        for i in range(3):
            remote(t_ref, block(0), ka_send.at[i], k_recv.at[0], w, x).wait_send()
        for i in range(3 * NX):
            remote(t_ref, block(0), kb_send.at[i], k_recv.at[0], w, x).wait_send()
    for copy in waits:
        copy.wait_recv()
    sends = waits
    total4 = g2[0]
    for n in range(1, NZ):
        total4 += g2[n]
    fin[...] = total4

    waits = []
    here = y * NC + c
    for n in (4, 5, 2, 3, 6, 7, 1):
        dy, dc = n // NC, n % NC
        copy = remote(
            fin, g3.at[here], p3_send.at[n], p3_recv.at[n], place(z, at_y(dy), c ^ dc), x
        )
        copy.start()
        waits.append(copy)
    g3[here] = total4
    for copy in sends:
        copy.wait_send()
    for copy in waits:
        copy.wait_recv()
    for n in range(NY * NC):
        out_ref[n * 4 : (n + 1) * 4, :] = g3[n]

    for copy in waits:
        copy.wait_send()


def local(three_center, occ_green, virt_green, occ_column, partner_live):
    t = three_center.reshape(AD, 8, 8, PB).transpose(0, 2, 1, 3).reshape(AD * BB, PB)
    occ = occ_green.transpose(0, 2, 3, 1).reshape(AD, BB, 32)
    virt = virt_green.transpose(0, 2, 3, 1).reshape(AD, BB, 32)
    vmem = pl.BlockSpec(memory_space=pltpu.VMEM)
    dma = pltpu.SemaphoreType.DMA
    return pl.pallas_call(
        kernel,
        out_shape=jax.ShapeDtypeStruct((32, PB), F32),
        in_specs=[pl.BlockSpec(memory_space=pltpu.HBM)] * 5,
        out_specs=vmem,
        scratch_shapes=[
            pltpu.VMEM((AD, BB, 32), BF16),
            pltpu.VMEM((AD, BB, 32), BF16),
            pltpu.VMEM((AD, 32), jnp.int32),
            pltpu.VMEM((AD, 32), jnp.int32),
            pltpu.VMEM((PEERS, 32, PB), BF16),
            pltpu.VMEM((PEERS, 32, PB), BF16),
            pltpu.VMEM((NY * AD * BB, PB), BF16),
            pltpu.VMEM((OWN, AD * BB, PB), BF16),
            pltpu.VMEM((PEERS, PB), jnp.int32),
            pltpu.SMEM((PEERS, PB), jnp.int32),
            pltpu.VMEM((16, CAP * PB, PB), BF16),
            pltpu.VMEM((PEERS * OWN, 8, PB), F32),
            pltpu.VMEM((PEERS * OWN, 8, PB), F32),
            pltpu.VMEM((AD * BB, PEERS * PB), BF16),
            pltpu.VMEM((AD * BB, PEERS * PB), BF16),
            pltpu.VMEM((PEERS * PB, PB), BF16),
            pltpu.VMEM((PEERS * PB, PB), BF16),
            pltpu.VMEM((OWN * AD * BB, PB), F32),
            pltpu.VMEM((NX, NY * NC, 4, PB), F32),
            pltpu.VMEM((PEERS * NC, 4, PB), F32),
            pltpu.VMEM((4, PB), F32),
            pltpu.VMEM((NZ, 4, PB), F32),
            pltpu.VMEM((4, PB), F32),
            pltpu.VMEM((NY * NC, 4, PB), F32),
            dma((PEERS,)), dma((PEERS,)),
            dma((NY,)), dma((NY,)),
            dma((NX,)), dma((3 * NX,)), dma((NX,)), dma((NX,)), dma((NX,)),
            dma((PEERS * NC,)), dma((PEERS * NC,)),
            dma((NZ,)), dma((NZ,)),
            dma((NY * NC,)), dma((NY * NC,)),
            dma((8,)),
        ],
        compiler_params=pltpu.CompilerParams(
            collective_id=0, has_side_effects=True, vmem_limit_bytes=32 * 1024 * 1024
        ),
    )(*[pltpu.with_memory_space_constraint(v, pltpu.HBM) for v in (t, occ, virt, occ_column, partner_live)])


def solution(mesh):
    placed = (
        P("wide", None, None),
        P("wide", "pair", None, None),
        P("wide", "pair", None, None),
        P("wide", "pair"),
        P("wide", "pair"),
    )
    return jax.shard_map(
        local, mesh=mesh, in_specs=placed, out_specs=P("pair", None), check_vma=False
    )
```
